32 devices in a mesh: dp: 8 (over z, y), ctx: 4 (over x, core).
Axes of the slice: x: 2, y: 2, z: 4, core: 2. Of those that a mesh axis runs over, the one named last changes fastest.
Arguments:
- queries: bfloat16 [8, 1024, 2048], P('dp', 'ctx'), may hold values from -20 to 20
- projected_keys: bfloat16 [8, 1024, 1024], P('dp', 'ctx'), may hold values from -6 to 6
- projected_values: bfloat16 [8, 1024, 1024], P('dp', 'ctx'), may hold values from -6 to 6
- attention_result: bfloat16 [8, 1024, 2048], P('dp', 'ctx'), may hold values from -3 to 3
- output_grad: bfloat16 [8, 1024, 5376], P('dp', 'ctx'), may hold values from -96 to 96
- out_weight: bfloat16 [2048, 5376], P('dp'), may hold values from -0.125 to 0.125
Outputs:
- query_grad: bfloat16 [8, 1024, 2048], P('dp', 'ctx')
- key_grad: bfloat16 [8, 1024, 1024], P('dp', 'ctx')
- value_grad: bfloat16 [8, 1024, 1024], P('dp', 'ctx')
The draws below stay inside these ranges and needn't reach their ends.
All inputs are finite; a program needn't handle non-finite values.
Results may differ from the reference program's by a relative error of at most 0.0061.
Values may be sent and summed in bfloat16 or wider, within the bound.
No kernel may reach another device: no remote copies, remote signals or barrier semaphores. Data moves between devices by JAX's collectives and lax.ppermute only.
A program may use at most 128 MiB of HBM per device.

```python
import jax
import jax.numpy as jnp
from jax import lax

D = 5376
HQ = 16
KEY_HEAD_COUNT = 8
HEAD_DIM = 128
WINDOW = 1024
SEQUENCE_TOKENS = 1024
SEQUENCE_COUNT = 8
QUERY_PER_KV = 2


def draw_queries(key, part):
    start_offset = jax.random.normal(jax.random.fold_in(key, 1), (SEQUENCE_COUNT, SEQUENCE_TOKENS, KEY_HEAD_COUNT, QUERY_PER_KV, HEAD_DIM), jnp.float32)
    start_offset = jnp.clip(start_offset, -6.0, 6.0)
    return start_offset.reshape(SEQUENCE_COUNT, SEQUENCE_TOKENS, HQ * HEAD_DIM).astype(jnp.bfloat16)


def draw_projected_keys(key, part):
    start_offset = jax.random.normal(jax.random.fold_in(key, 2), (SEQUENCE_COUNT, SEQUENCE_TOKENS, KEY_HEAD_COUNT, HEAD_DIM), jnp.float32)
    start_offset = jnp.clip(start_offset, -6.0, 6.0)
    return start_offset.reshape(SEQUENCE_COUNT, SEQUENCE_TOKENS, KEY_HEAD_COUNT * HEAD_DIM).astype(jnp.bfloat16)


def block_scale(stream_key, shape, split, smallest, high):
    level, own = 1.0, jax.random.fold_in(stream_key, 6)
    for axis_at, shards_of in split:
        steps = jnp.exp(jax.random.uniform(jax.random.fold_in(own, axis_at), (shards_of,), jnp.float32, smallest / len(split), high / len(split)))
        level = level * jnp.repeat(steps, shape[axis_at] // shards_of).reshape([-1 if axis == axis_at else 1 for axis in range(len(shape))])
    return level


def centred(own_key, shape, scale, most, shards=(), kind=jnp.bfloat16):
    entries = jax.random.normal(own_key, shape, jnp.float32) * scale
    if len(shards) > 0:
        entries = block_scale(own_key, shape, shards, -0.22, 0.18) * entries
    return jnp.clip(entries, min=-most, max=most).astype(kind)


def setup_inputs(seed: int = 0) -> dict:
    streams_of = jax.random.split(jax.random.key(seed), 7)
    queries = draw_queries(jax.random.fold_in(streams_of[6], 71), 0)
    projected_keys = draw_projected_keys(jax.random.fold_in(streams_of[6], 71), 0)
    projected_values = centred(streams_of[2], (SEQUENCE_COUNT, SEQUENCE_TOKENS, KEY_HEAD_COUNT * HEAD_DIM), 1.0, 6.0, ((0, 8), (1, 4)))
    attention_result = centred(streams_of[3], (SEQUENCE_COUNT, SEQUENCE_TOKENS, HQ * HEAD_DIM), 0.5, 3.0, ((0, 8), (1, 4)))
    output_grad = centred(streams_of[4], (SEQUENCE_COUNT, SEQUENCE_TOKENS, D), 16.0, 96.0, ((0, 8), (1, 4)))
    out_weight = centred(streams_of[5], (HQ * HEAD_DIM, D), (HQ * HEAD_DIM) ** -0.5, 0.125, ((0, 8),))
    return {"queries": queries, "projected_keys": projected_keys, "projected_values": projected_values, "attention_result": attention_result, "output_grad": output_grad, "out_weight": out_weight}


score_scale = 168.0 ** -0.5
masked_value = -1.0e30


def band_backward(query_head_total, key_head_total, value_head_total, gradient_by_head, delta_heads):
    sequence_tokens, local_kv, query_feature_width = query_head_total.shape
    head_size = key_head_total.shape[2]
    queries_per_group = query_feature_width // head_size
    block_rows = min(512, sequence_tokens)
    span_len = WINDOW + block_rows
    query_four = query_head_total.reshape(sequence_tokens, local_kv, queries_per_group, head_size).astype(jnp.float32)
    gradient_rank_four = gradient_by_head.reshape(sequence_tokens, local_kv, queries_per_group, head_size).astype(jnp.float32)
    leading = jnp.zeros((WINDOW, local_kv, head_size), jnp.float32)
    key_padded = jnp.concatenate([leading, key_head_total.astype(jnp.float32)], axis=0)
    value_padded = jnp.concatenate([leading, value_head_total.astype(jnp.float32)], axis=0)
    delta_float = delta_heads.astype(jnp.float32)

    def one_block(block_index, totals):
        query_total, key_total, value_total = totals
        first_row = (block_index * block_rows).astype(jnp.int32)
        query_block = lax.dynamic_slice_in_dim(query_four, first_row, block_rows, 0)
        grad_block = lax.dynamic_slice_in_dim(gradient_rank_four, first_row, block_rows, 0)
        delta_block = lax.dynamic_slice_in_dim(delta_float, first_row, block_rows, 0)
        key_block = lax.dynamic_slice_in_dim(key_padded, first_row, span_len, 0)
        value_block = lax.dynamic_slice_in_dim(value_padded, first_row, span_len, 0)
        scores = jnp.einsum("qhgd,khd->hgqk", query_block, key_block) * score_scale
        query_pos = first_row + lax.iota(jnp.int32, block_rows)
        key_pos = first_row - WINDOW + lax.iota(jnp.int32, span_len)
        visible = (key_pos[None, :] <= query_pos[:, None]) & (key_pos[None, :] > query_pos[:, None] - WINDOW) & (key_pos[None, :] >= 0)
        scores = jnp.where(visible, scores, masked_value)
        highest = jnp.max(scores, axis=-1, keepdims=True)
        expos = jnp.exp(scores - highest)
        probs = expos / jnp.sum(expos, axis=-1, keepdims=True)
        probs_low = probs.astype(jnp.bfloat16).astype(jnp.float32)
        dprobs = jnp.einsum("qhgd,khd->hgqk", grad_block, value_block)
        delta_rows = jnp.transpose(delta_block, (1, 2, 0))[..., None]
        dscores = (probs * (dprobs - delta_rows)).astype(jnp.bfloat16).astype(jnp.float32)
        query_part = jnp.einsum("hgqk,khd->qhgd", dscores, key_block) * score_scale
        key_portion = jnp.einsum("hgqk,qhgd->khd", dscores, query_block) * score_scale
        value_portion = jnp.einsum("hgqk,qhgd->khd", probs_low, grad_block)
        query_total = lax.dynamic_update_slice_in_dim(query_total, query_part.reshape(block_rows, local_kv, query_feature_width), first_row, 0)
        key_total = lax.dynamic_update_slice_in_dim(key_total, lax.dynamic_slice_in_dim(key_total, first_row, span_len, 0) + key_portion, first_row, 0)
        value_total = lax.dynamic_update_slice_in_dim(value_total, lax.dynamic_slice_in_dim(value_total, first_row, span_len, 0) + value_portion, first_row, 0)
        return (query_total, key_total, value_total)

    initial = (jnp.zeros((sequence_tokens, local_kv, query_feature_width), jnp.float32),
               jnp.zeros((WINDOW + sequence_tokens, local_kv, head_size), jnp.float32),
               jnp.zeros((WINDOW + sequence_tokens, local_kv, head_size), jnp.float32))
    query_total, key_total, value_total = lax.fori_loop(0, sequence_tokens // block_rows, one_block, initial)
    return (query_total.astype(jnp.bfloat16), key_total[WINDOW:].astype(jnp.bfloat16), value_total[WINDOW:].astype(jnp.bfloat16))


def reference(queries, projected_keys, projected_values, attention_result, output_grad, out_weight):
    def per_sequence(inputs):
        query_row_list, key_row_list, value_row_list, output_row_list, grad_rows = inputs
        sequence_tokens = query_row_list.shape[0]
        per_head_gradient = jnp.dot(grad_rows, out_weight.T, preferred_element_type=jnp.float32).astype(jnp.bfloat16)
        gradient_rank_four = per_head_gradient.reshape(sequence_tokens, KEY_HEAD_COUNT, QUERY_PER_KV, HEAD_DIM)
        output_rank_four = output_row_list.reshape(sequence_tokens, KEY_HEAD_COUNT, QUERY_PER_KV, HEAD_DIM)
        delta = jnp.sum(gradient_rank_four.astype(jnp.float32) * output_rank_four.astype(jnp.float32), axis=-1).astype(jnp.bfloat16)
        query_head_total = jnp.moveaxis(query_row_list.reshape(sequence_tokens, KEY_HEAD_COUNT, QUERY_PER_KV * HEAD_DIM), 1, 0)
        key_head_total = jnp.moveaxis(key_row_list.reshape(sequence_tokens, KEY_HEAD_COUNT, HEAD_DIM), 1, 0)
        value_head_total = jnp.moveaxis(value_row_list.reshape(sequence_tokens, KEY_HEAD_COUNT, HEAD_DIM), 1, 0)
        gradient_by_head = jnp.moveaxis(per_head_gradient.reshape(sequence_tokens, KEY_HEAD_COUNT, QUERY_PER_KV * HEAD_DIM), 1, 0)
        delta_heads = jnp.moveaxis(delta, 1, 0)

        def per_head(head_inputs):
            query_one, key_one, value_one, grad_one, delta_one = head_inputs
            return band_backward(query_one[:, None], key_one[:, None], value_one[:, None], grad_one[:, None], delta_one[:, None])

        query_part, key_portion, value_portion = lax.map(per_head, (query_head_total, key_head_total, value_head_total, gradient_by_head, delta_heads))
        query_out = jnp.moveaxis(query_part[:, :, 0], 0, 1).reshape(sequence_tokens, HQ * HEAD_DIM)
        key_gradient_out = jnp.moveaxis(key_portion[:, :, 0], 0, 1).reshape(sequence_tokens, KEY_HEAD_COUNT * HEAD_DIM)
        value_gradient_out = jnp.moveaxis(value_portion[:, :, 0], 0, 1).reshape(sequence_tokens, KEY_HEAD_COUNT * HEAD_DIM)
        return (query_out, key_gradient_out, value_gradient_out)

    query_grad, key_grad, value_grad = lax.map(per_sequence, (queries, projected_keys, projected_values, attention_result, output_grad))
    return query_grad, key_grad, value_grad
```

```python
import functools

import jax
import jax.numpy as jnp
from jax import lax
from jax.experimental import pallas as pl
from jax.experimental.pallas import tpu as pltpu
from jax.sharding import PartitionSpec as P

KEY_HEAD_COUNT = 8
HEAD_DIM = 128
WINDOW = 1024


score_scale = 168.0 ** (-0.5)
masked_value = -1e30


def band_backward(
    query_head_total, key_head_total, value_head_total, gradient_by_head, delta_heads
):
    sequence_tokens, local_kv, query_feature_width = query_head_total.shape
    head_size = key_head_total.shape[2]
    queries_per_group = query_feature_width // head_size
    block_rows = min(512, sequence_tokens)
    span_len = WINDOW + block_rows
    query_four = query_head_total.reshape(sequence_tokens, local_kv, queries_per_group, head_size)
    gradient_rank_four = gradient_by_head.reshape(
        sequence_tokens, local_kv, queries_per_group, head_size
    )
    leading = jnp.zeros((WINDOW, local_kv, head_size), key_head_total.dtype)
    key_padded = jnp.concatenate([leading, key_head_total], axis=0)
    value_padded = jnp.concatenate([leading, value_head_total], axis=0)
    delta_float = delta_heads.astype(jnp.float32)

    def one_block(block_index, totals):
        query_total, key_total, value_total = totals
        first_row = (block_index * block_rows).astype(jnp.int32)
        query_block = lax.dynamic_slice_in_dim(query_four, first_row, block_rows, 0)
        grad_block = lax.dynamic_slice_in_dim(gradient_rank_four, first_row, block_rows, 0)
        delta_block = lax.dynamic_slice_in_dim(delta_float, first_row, block_rows, 0)
        key_block = lax.dynamic_slice_in_dim(key_padded, first_row, span_len, 0)
        value_block = lax.dynamic_slice_in_dim(value_padded, first_row, span_len, 0)
        scores = (
            jnp.einsum("qhgd,khd->hgqk", query_block, key_block, preferred_element_type=jnp.float32)
            * score_scale
        )
        query_pos = first_row + lax.iota(jnp.int32, block_rows)
        key_pos = first_row - WINDOW + lax.iota(jnp.int32, span_len)
        visible = (
            (key_pos[None, :] <= query_pos[:, None])
            & (key_pos[None, :] > query_pos[:, None] - WINDOW)
            & (key_pos[None, :] >= 0)
        )
        scores = jnp.where(visible, scores, masked_value)
        highest = jnp.max(scores, axis=-1, keepdims=True)
        expos = jnp.exp(scores - highest)
        probs = expos / jnp.sum(expos, axis=-1, keepdims=True)
        probs_low = probs.astype(jnp.bfloat16)
        dprobs = jnp.einsum(
            "qhgd,khd->hgqk", grad_block, value_block, preferred_element_type=jnp.float32
        )
        delta_rows = jnp.transpose(delta_block, (1, 2, 0))[..., None]
        dscores = (probs * (dprobs - delta_rows)).astype(jnp.bfloat16)
        query_part = (
            jnp.einsum("hgqk,khd->qhgd", dscores, key_block, preferred_element_type=jnp.float32)
            * score_scale
        )
        key_portion = (
            jnp.einsum("hgqk,qhgd->khd", dscores, query_block, preferred_element_type=jnp.float32)
            * score_scale
        )
        value_portion = jnp.einsum(
            "hgqk,qhgd->khd", probs_low, grad_block, preferred_element_type=jnp.float32
        )
        query_total = lax.dynamic_update_slice_in_dim(
            query_total, query_part.reshape(block_rows, local_kv, query_feature_width), first_row, 0
        )
        key_total = lax.dynamic_update_slice_in_dim(
            key_total,
            lax.dynamic_slice_in_dim(key_total, first_row, span_len, 0) + key_portion,
            first_row,
            0,
        )
        value_total = lax.dynamic_update_slice_in_dim(
            value_total,
            lax.dynamic_slice_in_dim(value_total, first_row, span_len, 0) + value_portion,
            first_row,
            0,
        )
        return (query_total, key_total, value_total)

    initial = (
        jnp.zeros((sequence_tokens, local_kv, query_feature_width), jnp.float32),
        jnp.zeros((WINDOW + sequence_tokens, local_kv, head_size), jnp.float32),
        jnp.zeros((WINDOW + sequence_tokens, local_kv, head_size), jnp.float32),
    )
    query_total, key_total, value_total = lax.fori_loop(
        0, sequence_tokens // block_rows, one_block, initial
    )
    return (
        query_total.astype(jnp.bfloat16),
        key_total[WINDOW:].astype(jnp.bfloat16),
        value_total[WINDOW:].astype(jnp.bfloat16),
    )


def head_delta(gradient_rank_three, output_rank_three):
    rows_here, heads_here, query_feature_width = gradient_rank_three.shape
    queries_per_group = query_feature_width // HEAD_DIM
    gradient_rank_four = gradient_rank_three.reshape(
        rows_here, heads_here, queries_per_group, HEAD_DIM
    ).astype(jnp.float32)
    output_rank_four = output_rank_three.reshape(
        rows_here, heads_here, queries_per_group, HEAD_DIM
    ).astype(jnp.float32)
    return jnp.sum(gradient_rank_four * output_rank_four, axis=-1).astype(jnp.bfloat16)


def one_sequence(query_rows, key_rows, value_rows, output_rows, gradient_rows):
    token_total = query_rows.shape[0]
    query_feature_width = query_rows.shape[1]
    queries_per_group = query_feature_width // (KEY_HEAD_COUNT * HEAD_DIM)
    query_rank_three = query_rows.reshape(token_total, KEY_HEAD_COUNT, queries_per_group * HEAD_DIM)
    key_rank_three = key_rows.reshape(token_total, KEY_HEAD_COUNT, HEAD_DIM)
    value_rank_three = value_rows.reshape(token_total, KEY_HEAD_COUNT, HEAD_DIM)
    output_rank_three = output_rows.reshape(
        token_total, KEY_HEAD_COUNT, queries_per_group * HEAD_DIM
    )
    gradient_rank_three = gradient_rows.reshape(
        token_total, KEY_HEAD_COUNT, queries_per_group * HEAD_DIM
    )
    query_head_total, key_head_total, value_head_total, output_heads = (
        lax.all_to_all(query_rank_three, "ctx", split_axis=1, concat_axis=0, tiled=True),
        lax.all_to_all(key_rank_three, "ctx", split_axis=1, concat_axis=0, tiled=True),
        lax.all_to_all(value_rank_three, "ctx", split_axis=1, concat_axis=0, tiled=True),
        lax.all_to_all(output_rank_three, "ctx", split_axis=1, concat_axis=0, tiled=True),
    )
    gradient_by_head = lax.all_to_all(
        gradient_rank_three, "ctx", split_axis=1, concat_axis=0, tiled=True
    )
    delta_heads = head_delta(gradient_by_head, output_heads)
    query_back, key_back, value_back = band_backward(
        query_head_total, key_head_total, value_head_total, gradient_by_head, delta_heads
    )
    query_local, key_slice_here, value_slice_here = (
        lax.all_to_all(query_back, "ctx", split_axis=0, concat_axis=1, tiled=True),
        lax.all_to_all(key_back, "ctx", split_axis=0, concat_axis=1, tiled=True),
        lax.all_to_all(value_back, "ctx", split_axis=0, concat_axis=1, tiled=True),
    )
    return (
        query_local.reshape(token_total, query_feature_width),
        key_slice_here.reshape(token_total, KEY_HEAD_COUNT * HEAD_DIM),
        value_slice_here.reshape(token_total, KEY_HEAD_COUNT * HEAD_DIM),
    )


def body(queries, projected_keys, projected_values, attention_result, output_grad, out_weight):
    sequences_here = queries.shape[0]
    token_total = queries.shape[1]
    query_feature_width = queries.shape[2]
    row_total = sequences_here * token_total
    grad_rows = output_grad.reshape(row_total, output_grad.shape[2])
    per_head_gradient = lax.dot_general(
        grad_rows,
        lax.all_gather(out_weight, "dp", axis=0, tiled=True),
        (((1,), (1,)), ((), ())),
        preferred_element_type=jnp.float32,
    ).astype(jnp.bfloat16)
    per_head_gradient = per_head_gradient.reshape(sequences_here, token_total, query_feature_width)
    query_part, key_part, value_part = one_sequence(
        queries[0],
        projected_keys[0],
        projected_values[0],
        attention_result[0],
        per_head_gradient[0],
    )
    query_list = [query_part]
    key_list = [key_part]
    value_list = [value_part]
    return (
        jnp.stack(query_list, axis=0),
        jnp.stack(key_list, axis=0),
        jnp.stack(value_list, axis=0),
    )


AXES = ("dp", "ctx")
SHARED_COLS = 640
BF = jnp.bfloat16
F32 = jnp.float32


def place(x, c, y, z):
    return (z * 2 + y) * 4 + x * 2 + c


def pairs(target):
    found = []
    for z in range(4):
        for y in range(2):
            for x in range(2):
                for c in range(2):
                    to = target(x, c, y, z)
                    if to is not None:
                        found.append((place(x, c, y, z), place(*to)))
    return found


def send(value, target):
    return lax.ppermute(value, AXES, pairs(target))


def over_x(x, c, y, z):
    return (1 - x, c, y, z)


def over_y(x, c, y, z):
    return (x, c, 1 - y, z)


def over_core(x, c, y, z):
    return (x, 1 - c, y, z)


def over_z(step):
    return lambda x, c, y, z: (x, c, y, z ^ step)


def nt(a, b):
    return lax.dot_general(a, b, (((1,), (1,)), ((), ())), preferred_element_type=F32)


def nn(a, b):
    return lax.dot_general(a, b, (((1,), (0,)), ((), ())), preferred_element_type=F32)


def tn(a, b):
    return lax.dot_general(a, b, (((0,), (0,)), ((), ())), preferred_element_type=F32)


def spec(shape, index):
    return pl.BlockSpec(shape, index)


def whole(shape):
    return pl.BlockSpec(shape, lambda *_: (0,) * len(shape))


VMEM_LIMIT = 56 * 1024 * 1024


def call(kernel, scalars, grid, in_specs, out_specs, out_shape, args, cost, name):
    return pl.pallas_call(
        kernel,
        grid_spec=pltpu.PrefetchScalarGridSpec(
            num_scalar_prefetch=1, grid=grid, in_specs=in_specs, out_specs=out_specs
        ),
        out_shape=out_shape,
        compiler_params=pltpu.CompilerParams(vmem_limit_bytes=VMEM_LIMIT),
        cost_estimate=pl.CostEstimate(flops=cost[0], transcendentals=0, bytes_accessed=cost[1]),
        name=name,
    )(scalars, *args)


def weight_rows_kernel(info, og_own, og_other, w_common, w_mine, w_other, out):
    x = info[0]
    c = info[1]
    cols = w_common.shape[1]
    rows = og_own.shape[0]
    first = w_common[pl.ds(pl.multiple_of(x * HEAD_DIM, HEAD_DIM), HEAD_DIM), :]
    second = w_common[pl.ds(pl.multiple_of((1 - x) * HEAD_DIM, HEAD_DIM), HEAD_DIM), :]
    common = jnp.concatenate([first, second], axis=0)
    rest = jnp.concatenate([w_mine[...], w_other[...]], axis=0)
    for og, block in ((og_own, c), (og_other, 1 - c)):
        total = nt(og[:, :cols], common) + nt(og[:, cols:], rest)
        out[pl.ds(pl.multiple_of(block * rows, rows), rows), :] = total.astype(out.dtype)


def head_part(info, og_own, og_other, w_common, w_mine, w_other, dtype, name):
    rows, half = og_own.shape
    flops = 4 * rows * half * 256
    return call(
        weight_rows_kernel,
        info,
        (1,),
        [whole(a.shape) for a in (og_own, og_other, w_common, w_mine, w_other)],
        whole((2 * rows, 256)),
        jax.ShapeDtypeStruct((2 * rows, 256), dtype),
        (og_own, og_other, w_common, w_mine, w_other),
        (flops, 2 * half * (2 * rows + 256)),
        name,
    )


def probs_kernel(info, q, kd, kx, pd, px):
    rows = q.shape[0]
    scale = score_scale
    row = lax.broadcasted_iota(jnp.int32, (rows, rows), 0)
    col = lax.broadcasted_iota(jnp.int32, (rows, rows), 1)
    seen = col <= row

    for head in range(2):
        query = q[:, head * HEAD_DIM : (head + 1) * HEAD_DIM]
        near = jnp.where(seen, nt(query, kd[...]) * scale, masked_value)

        @pl.when(info[0] == 0)
        def _():
            high = jnp.max(near, axis=-1, keepdims=True)
            near_exp = jnp.exp(near - high)
            total = jnp.sum(near_exp, axis=-1, keepdims=True)
            pd[0, head] = (near_exp * (1.0 / total)).astype(BF)

        @pl.when(info[0] == 1)
        def _():
            far = nt(query, kx[...]) * scale
            high = jnp.maximum(
                jnp.max(near, axis=-1, keepdims=True), jnp.max(far, axis=-1, keepdims=True)
            )
            near_exp = jnp.exp(near - high)
            far_exp = jnp.exp(far - high)
            total = jnp.sum(near_exp, axis=-1, keepdims=True) + jnp.sum(
                far_exp, axis=-1, keepdims=True
            )
            inverse = 1.0 / total
            pd[0, head] = (near_exp * inverse).astype(BF)
            px[0, head] = (far_exp * inverse).astype(BF)


def all_probs(info, q, kd, kx):
    rows = q.shape[0]
    slots = q.shape[1] // 256
    shape = jax.ShapeDtypeStruct((slots, 2, rows, rows), BF)
    prob_spec = spec((1, 2, rows, rows), lambda s, info: (s, 0, 0, 0))
    key_spec = spec((rows, HEAD_DIM), lambda s, info: (0, s))
    return call(
        probs_kernel,
        info,
        (slots,),
        [spec((rows, 256), lambda s, info: (0, s)), key_spec, key_spec],
        [prob_spec, prob_spec],
        [shape, shape],
        (q, kd, kx),
        (slots * 2 * rows * rows * 512, slots * 4 * rows * rows * 4),
        "probs",
    )


def grads_kernel(info, own, back, out, q, kd, vd, kx, vx, pd, px, dq, near, far):
    x = info[0]
    step = pl.program_id(0)
    scale = score_scale
    head_grad = (own[...] + back[...].astype(F32)).astype(BF)
    query = q[...]
    delta = jnp.sum(head_grad.astype(F32) * out[...].astype(F32), axis=-1, keepdims=True)
    delta = delta.astype(BF).astype(F32)
    prob = pd[0, 0]
    dscore = (prob.astype(F32) * (nt(head_grad, vd[...]) - delta)).astype(BF)
    dkey = tn(dscore, query) * scale
    dvalue = tn(prob, head_grad)

    @pl.when(step == 0)
    def _():
        near[:, :HEAD_DIM] = dkey
        near[:, HEAD_DIM:] = dvalue

    @pl.when(step == 1)
    def _():
        near[:, :HEAD_DIM] += dkey
        near[:, HEAD_DIM:] += dvalue

    dquery = nn(dscore, kd[...])

    @pl.when(x == 0)
    def _():
        dq[...] = (dquery * scale).astype(BF)

    @pl.when(x == 1)
    def _():
        prob_far = px[0, 0]
        dscore_far = (prob_far.astype(F32) * (nt(head_grad, vx[...]) - delta)).astype(BF)
        dq[...] = ((dquery + nn(dscore_far, kx[...])) * scale).astype(BF)
        dkey_far = tn(dscore_far, query) * scale
        dvalue_far = tn(prob_far, head_grad)

        @pl.when(step == 0)
        def _():
            far[:, :HEAD_DIM] = dkey_far
            far[:, HEAD_DIM:] = dvalue_far

        @pl.when(step == 1)
        def _():
            far[:, :HEAD_DIM] += dkey_far
            far[:, HEAD_DIM:] += dvalue_far


def head_grads(info, own, back, out, q, kd, vd, kx, vx, pd, px, name):
    rows = q.shape[0]

    def wide(i, info):
        return (0, 2 * info[2] + (i ^ info[0]))

    def plane(i, info):
        return (0, i)

    def key(i, info):
        return (0, info[2])

    def prob(i, info):
        return (info[2], i ^ info[0], 0, 0)

    narrow = (rows, HEAD_DIM)
    return call(
        grads_kernel,
        info,
        (2,),
        [
            spec(narrow, plane),
            spec(narrow, plane),
            spec(narrow, wide),
            spec(narrow, wide),
            spec(narrow, key),
            spec(narrow, key),
            spec(narrow, key),
            spec(narrow, key),
            spec((1, 1, rows, rows), prob),
            spec((1, 1, rows, rows), prob),
        ],
        [
            spec(narrow, lambda i, info: (0, i ^ info[0])),
            whole((rows, 256)),
            whole((rows, 256)),
        ],
        [
            jax.ShapeDtypeStruct((rows, 256), BF),
            jax.ShapeDtypeStruct((rows, 256), F32),
            jax.ShapeDtypeStruct((rows, 256), F32),
        ],
        (own, back, out, q, kd, vd, kx, vx, pd, px),
        (2 * 8 * 2 * rows * rows * HEAD_DIM, 4 * rows * rows * 2 + 8 * rows * 256 * 2),
        name,
    )


def finish_kernel(info, *refs):
    steps = len(refs[:-3]) // 3
    query_out, key_out, value_out = refs[-3:]
    c = info[1]
    z = info[2]
    for r in range(steps):
        dq, dkv, other = refs[3 * r : 3 * r + 3]
        slot = z ^ r
        mine = 2 * slot + c
        theirs = 2 * slot + 1 - c
        wide = lambda g: pl.ds(pl.multiple_of(g * 256, 256), 256)
        thin = lambda g: pl.ds(pl.multiple_of(g * HEAD_DIM, HEAD_DIM), HEAD_DIM)
        query_out[:, wide(mine)] = dq[...]
        key_out[:, thin(mine)] = dkv[:, :HEAD_DIM]
        value_out[:, thin(mine)] = dkv[:, HEAD_DIM:]
        query_out[:, wide(theirs)] = other[:, :256]
        key_out[:, thin(theirs)] = other[:, 256 : 256 + HEAD_DIM]
        value_out[:, thin(theirs)] = other[:, 256 + HEAD_DIM :]


def fast_body(queries, projected_keys, projected_values, attention_result, output_grad, out_weight):
    q, k, v, o, og = (
        a[0]
        for a in (queries, projected_keys, projected_values, attention_result, output_grad)
    )
    rows = q.shape[0]
    half = og.shape[1] // 2
    shared = SHARED_COLS
    dp = lax.axis_index("dp")
    ctx = lax.axis_index("ctx")
    z, y = dp // 2, dp % 2
    x, c = ctx // 2, ctx % 2
    info = jnp.stack([x, c, z]).astype(jnp.int32)

    w_cross_common = lax.dynamic_slice(out_weight, (0, (1 - y) * half), (256, shared))
    w_cross_mine = lax.dynamic_slice(
        out_weight, (x * HEAD_DIM, (1 - y) * half + shared), (HEAD_DIM, half - shared)
    )
    to_other = lambda x, c, y, z: (x, c, 1 - y, z) if y == c else None
    got_mine = send(w_cross_mine, to_other)
    got_common = send(w_cross_common, to_other)
    own_here = y == c
    base_mine = jnp.where(
        own_here,
        lax.dynamic_slice(out_weight, (x * HEAD_DIM, y * half + shared), (HEAD_DIM, half - shared)),
        got_mine,
    )
    base_common = jnp.where(
        own_here, lax.dynamic_slice(out_weight, (0, y * half), (256, shared)), got_common
    )
    mine = [base_mine]
    common = [base_common]
    for step in (1, 2):
        mine.append(send(base_mine, over_z(step)))
        common.append(send(base_common, over_z(step)))
    mine.append(send(mine[2], over_z(1)))
    common.append(send(common[2], over_z(1)))

    og_keep = lax.dynamic_slice(og, (0, y * half), (rows, half))
    og_send = lax.dynamic_slice(og, (0, (1 - y) * half), (rows, half))
    og_keep_core = send(og_keep, over_core)
    og_back = send(og_send, over_y)
    og_back_core = send(og_back, over_core)

    def parts(a, width):
        a = a.reshape(rows, 4, 2, width)
        take = lambda i: lax.dynamic_index_in_dim(a, i, 2, keepdims=False).reshape(rows, 4 * width)
        return take(c), take(1 - c)

    def ordered(first, second):
        return jnp.concatenate(
            [jnp.where(c == 0, first, second), jnp.where(c == 0, second, first)], axis=0
        )

    def gather(a, width):
        keep, give = parts(a, width)
        return ordered(keep, send(give, over_core))

    q_chip = gather(q, 256)
    k_chip = gather(k, HEAD_DIM)
    v_chip = gather(v, HEAD_DIM)
    o_chip = gather(o, 256)
    forward = lambda x, c, y, z: (1, c, y, z) if x == 0 else None
    backward = lambda x, c, y, z: (0, c, y, z) if x == 1 else None
    k_far = send(k_chip, forward)
    v_far = send(v_chip, forward)
    probs_near, probs_far = all_probs(info, q_chip, k_chip, k_far)

    finals = []
    for r in range(4):
        other = send(mine[r], over_x)
        part = head_part(info, og_back, og_back_core, common[r], mine[r], other, BF, f"give{r}")
        back = send(part, over_y)
        own = head_part(info, og_keep, og_keep_core, common[r], mine[r], other, F32, f"keep{r}")
        slot = jnp.stack([x, c, z ^ r]).astype(jnp.int32)
        dq, near, far = head_grads(
            slot, own, back, o_chip, q_chip, k_chip, v_chip, k_far, v_far,
            probs_near, probs_far, f"grads{r}",
        )
        from_far = send(far.astype(BF), backward)
        dkv = (near + from_far.astype(F32)).astype(BF)
        pick = lambda a, i: lax.dynamic_slice(a, (i * rows, 0), (rows, a.shape[1]))
        crossed = send(
            jnp.concatenate([pick(dq, 1 - c), pick(dkv, 1 - c)], axis=1), over_core
        )
        finals += [dq, dkv, crossed]

    in_specs = []
    for r in range(4):
        mine_spec = spec((rows, 256), lambda i, info: (info[1], 0))
        in_specs += [mine_spec, mine_spec, whole((rows, 512))]
    outs = call(
        finish_kernel,
        info,
        (1,),
        in_specs,
        [whole(a.shape) for a in (q, k, v)],
        [jax.ShapeDtypeStruct(a.shape, BF) for a in (q, k, v)],
        finals,
        (0, 4 * rows * 4096),
        "finish",
    )
    return tuple(a[None] for a in outs)


def fits_fast(mesh):
    return dict(mesh.shape) == {"dp": 8, "ctx": 4}


def chosen_body(mesh):
    def run(queries, projected_keys, projected_values, attention_result, output_grad, out_weight):
        fast = (
            fits_fast(mesh)
            and queries.shape == (1, 256, 2048)
            and out_weight.shape[0] == 256
            and projected_keys.shape == (1, 256, 1024)
            and output_grad.shape[2] % 256 == 0
        )
        use = fast_body if fast else body
        return use(
            queries, projected_keys, projected_values, attention_result, output_grad, out_weight
        )

    return run


def solution(mesh):
    placed = (
        P("dp", "ctx", None),
        P("dp", "ctx", None),
        P("dp", "ctx", None),
        P("dp", "ctx", None),
        P("dp", "ctx", None),
        P("dp", None),
    )
    return jax.shard_map(
        chosen_body(mesh),
        mesh=mesh,
        in_specs=placed,
        out_specs=(P("dp", "ctx", None), P("dp", "ctx", None), P("dp", "ctx", None)),
        check_vma=False,
    )
```

```python
import functools

import jax
import jax.numpy as jnp
from jax import lax
from jax.experimental import pallas as pl
from jax.experimental.pallas import tpu as pltpu
from jax.sharding import PartitionSpec as P

KEY_HEAD_COUNT = 8
HEAD_DIM = 128
WINDOW = 1024


score_scale = 168.0 ** (-0.5)
masked_value = -1e30


def band_backward(
    query_head_total, key_head_total, value_head_total, gradient_by_head, delta_heads
):
    sequence_tokens, local_kv, query_feature_width = query_head_total.shape
    head_size = key_head_total.shape[2]
    queries_per_group = query_feature_width // head_size
    block_rows = min(512, sequence_tokens)
    span_len = WINDOW + block_rows
    query_four = query_head_total.reshape(sequence_tokens, local_kv, queries_per_group, head_size)
    gradient_rank_four = gradient_by_head.reshape(
        sequence_tokens, local_kv, queries_per_group, head_size
    )
    leading = jnp.zeros((WINDOW, local_kv, head_size), key_head_total.dtype)
    key_padded = jnp.concatenate([leading, key_head_total], axis=0)
    value_padded = jnp.concatenate([leading, value_head_total], axis=0)
    delta_float = delta_heads.astype(jnp.float32)

    def one_block(block_index, totals):
        query_total, key_total, value_total = totals
        first_row = (block_index * block_rows).astype(jnp.int32)
        query_block = lax.dynamic_slice_in_dim(query_four, first_row, block_rows, 0)
        grad_block = lax.dynamic_slice_in_dim(gradient_rank_four, first_row, block_rows, 0)
        delta_block = lax.dynamic_slice_in_dim(delta_float, first_row, block_rows, 0)
        key_block = lax.dynamic_slice_in_dim(key_padded, first_row, span_len, 0)
        value_block = lax.dynamic_slice_in_dim(value_padded, first_row, span_len, 0)
        scores = (
            jnp.einsum("qhgd,khd->hgqk", query_block, key_block, preferred_element_type=jnp.float32)
            * score_scale
        )
        query_pos = first_row + lax.iota(jnp.int32, block_rows)
        key_pos = first_row - WINDOW + lax.iota(jnp.int32, span_len)
        visible = (
            (key_pos[None, :] <= query_pos[:, None])
            & (key_pos[None, :] > query_pos[:, None] - WINDOW)
            & (key_pos[None, :] >= 0)
        )
        scores = jnp.where(visible, scores, masked_value)
        highest = jnp.max(scores, axis=-1, keepdims=True)
        expos = jnp.exp(scores - highest)
        probs = expos / jnp.sum(expos, axis=-1, keepdims=True)
        probs_low = probs.astype(jnp.bfloat16)
        dprobs = jnp.einsum(
            "qhgd,khd->hgqk", grad_block, value_block, preferred_element_type=jnp.float32
        )
        delta_rows = jnp.transpose(delta_block, (1, 2, 0))[..., None]
        dscores = (probs * (dprobs - delta_rows)).astype(jnp.bfloat16)
        query_part = (
            jnp.einsum("hgqk,khd->qhgd", dscores, key_block, preferred_element_type=jnp.float32)
            * score_scale
        )
        key_portion = (
            jnp.einsum("hgqk,qhgd->khd", dscores, query_block, preferred_element_type=jnp.float32)
            * score_scale
        )
        value_portion = jnp.einsum(
            "hgqk,qhgd->khd", probs_low, grad_block, preferred_element_type=jnp.float32
        )
        query_total = lax.dynamic_update_slice_in_dim(
            query_total, query_part.reshape(block_rows, local_kv, query_feature_width), first_row, 0
        )
        key_total = lax.dynamic_update_slice_in_dim(
            key_total,
            lax.dynamic_slice_in_dim(key_total, first_row, span_len, 0) + key_portion,
            first_row,
            0,
        )
        value_total = lax.dynamic_update_slice_in_dim(
            value_total,
            lax.dynamic_slice_in_dim(value_total, first_row, span_len, 0) + value_portion,
            first_row,
            0,
        )
        return (query_total, key_total, value_total)

    initial = (
        jnp.zeros((sequence_tokens, local_kv, query_feature_width), jnp.float32),
        jnp.zeros((WINDOW + sequence_tokens, local_kv, head_size), jnp.float32),
        jnp.zeros((WINDOW + sequence_tokens, local_kv, head_size), jnp.float32),
    )
    query_total, key_total, value_total = lax.fori_loop(
        0, sequence_tokens // block_rows, one_block, initial
    )
    return (
        query_total.astype(jnp.bfloat16),
        key_total[WINDOW:].astype(jnp.bfloat16),
        value_total[WINDOW:].astype(jnp.bfloat16),
    )


def head_delta(gradient_rank_three, output_rank_three):
    rows_here, heads_here, query_feature_width = gradient_rank_three.shape
    queries_per_group = query_feature_width // HEAD_DIM
    gradient_rank_four = gradient_rank_three.reshape(
        rows_here, heads_here, queries_per_group, HEAD_DIM
    ).astype(jnp.float32)
    output_rank_four = output_rank_three.reshape(
        rows_here, heads_here, queries_per_group, HEAD_DIM
    ).astype(jnp.float32)
    return jnp.sum(gradient_rank_four * output_rank_four, axis=-1).astype(jnp.bfloat16)


def one_sequence(query_rows, key_rows, value_rows, output_rows, gradient_rows):
    token_total = query_rows.shape[0]
    query_feature_width = query_rows.shape[1]
    queries_per_group = query_feature_width // (KEY_HEAD_COUNT * HEAD_DIM)
    query_rank_three = query_rows.reshape(token_total, KEY_HEAD_COUNT, queries_per_group * HEAD_DIM)
    key_rank_three = key_rows.reshape(token_total, KEY_HEAD_COUNT, HEAD_DIM)
    value_rank_three = value_rows.reshape(token_total, KEY_HEAD_COUNT, HEAD_DIM)
    output_rank_three = output_rows.reshape(
        token_total, KEY_HEAD_COUNT, queries_per_group * HEAD_DIM
    )
    gradient_rank_three = gradient_rows.reshape(
        token_total, KEY_HEAD_COUNT, queries_per_group * HEAD_DIM
    )
    query_head_total, key_head_total, value_head_total, output_heads = (
        lax.all_to_all(query_rank_three, "ctx", split_axis=1, concat_axis=0, tiled=True),
        lax.all_to_all(key_rank_three, "ctx", split_axis=1, concat_axis=0, tiled=True),
        lax.all_to_all(value_rank_three, "ctx", split_axis=1, concat_axis=0, tiled=True),
        lax.all_to_all(output_rank_three, "ctx", split_axis=1, concat_axis=0, tiled=True),
    )
    gradient_by_head = lax.all_to_all(
        gradient_rank_three, "ctx", split_axis=1, concat_axis=0, tiled=True
    )
    delta_heads = head_delta(gradient_by_head, output_heads)
    query_back, key_back, value_back = band_backward(
        query_head_total, key_head_total, value_head_total, gradient_by_head, delta_heads
    )
    query_local, key_slice_here, value_slice_here = (
        lax.all_to_all(query_back, "ctx", split_axis=0, concat_axis=1, tiled=True),
        lax.all_to_all(key_back, "ctx", split_axis=0, concat_axis=1, tiled=True),
        lax.all_to_all(value_back, "ctx", split_axis=0, concat_axis=1, tiled=True),
    )
    return (
        query_local.reshape(token_total, query_feature_width),
        key_slice_here.reshape(token_total, KEY_HEAD_COUNT * HEAD_DIM),
        value_slice_here.reshape(token_total, KEY_HEAD_COUNT * HEAD_DIM),
    )


def body(queries, projected_keys, projected_values, attention_result, output_grad, out_weight):
    sequences_here = queries.shape[0]
    token_total = queries.shape[1]
    query_feature_width = queries.shape[2]
    row_total = sequences_here * token_total
    grad_rows = output_grad.reshape(row_total, output_grad.shape[2])
    per_head_gradient = lax.dot_general(
        grad_rows,
        lax.all_gather(out_weight, "dp", axis=0, tiled=True),
        (((1,), (1,)), ((), ())),
        preferred_element_type=jnp.float32,
    ).astype(jnp.bfloat16)
    per_head_gradient = per_head_gradient.reshape(sequences_here, token_total, query_feature_width)
    query_part, key_part, value_part = one_sequence(
        queries[0],
        projected_keys[0],
        projected_values[0],
        attention_result[0],
        per_head_gradient[0],
    )
    query_list = [query_part]
    key_list = [key_part]
    value_list = [value_part]
    return (
        jnp.stack(query_list, axis=0),
        jnp.stack(key_list, axis=0),
        jnp.stack(value_list, axis=0),
    )


AXES = ("dp", "ctx")
SHARED_COLS = 640
BF = jnp.bfloat16
F32 = jnp.float32


def place(x, c, y, z):
    return (z * 2 + y) * 4 + x * 2 + c


def pairs(target):
    found = []
    for z in range(4):
        for y in range(2):
            for x in range(2):
                for c in range(2):
                    to = target(x, c, y, z)
                    if to is not None:
                        found.append((place(x, c, y, z), place(*to)))
    return found


def send(value, target):
    return lax.ppermute(value, AXES, pairs(target))


def over_x(x, c, y, z):
    return (1 - x, c, y, z)


def over_y(x, c, y, z):
    return (x, c, 1 - y, z)


def over_core(x, c, y, z):
    return (x, 1 - c, y, z)


def over_z(step):
    return lambda x, c, y, z: (x, c, y, z ^ step)


def nt(a, b):
    return lax.dot_general(a, b, (((1,), (1,)), ((), ())), preferred_element_type=F32)


def nn(a, b):
    return lax.dot_general(a, b, (((1,), (0,)), ((), ())), preferred_element_type=F32)


def tn(a, b):
    return lax.dot_general(a, b, (((0,), (0,)), ((), ())), preferred_element_type=F32)


def near_call(kernel, info, args, outs, limit, in_hbm=False, out_hbm=False, scratch=()):
    vmem = pl.BlockSpec(memory_space=pltpu.VMEM)
    wide = pl.BlockSpec(memory_space=pltpu.HBM)
    if not in_hbm:
        args = [pltpu.with_memory_space_constraint(a, pltpu.VMEM) for a in args]
    shapes = [
        jax.ShapeDtypeStruct(s, d) if out_hbm else pltpu.VMEM(s, d) for s, d in outs
    ]
    return pl.pallas_call(
        kernel,
        in_specs=[pl.BlockSpec(memory_space=pltpu.SMEM)]
        + [wide if in_hbm else vmem] * len(args),
        out_specs=[vmem] * len(outs),
        out_shape=shapes,
        scratch_shapes=list(scratch),
        compiler_params=pltpu.CompilerParams(vmem_limit_bytes=limit * 1024 * 1024),
    )(info, *args)


def lanes(start, size):
    return pl.ds(pl.multiple_of(start, HEAD_DIM), size)


def split_weights_kernel(info, weight, cross, own, sem):
    x, y = info[0], info[2]
    width = own.shape[1]
    half = weight.shape[1] // 2
    shared = SHARED_COLS
    rest = half - shared
    jobs = []
    for out, side in ((cross, 1 - y), (own, y)):
        first = side * half
        jobs.append((weight.at[lanes(x * 128, 128), lanes(first + shared, rest)], out.at[:, :rest]))
        jobs.append((weight.at[0:128, lanes(first, shared)], out.at[:, rest : rest + shared]))
        jobs.append((weight.at[128:256, lanes(first, shared)], out.at[:, rest + shared : width]))
    copies = [pltpu.make_async_copy(s, d, sem.at[i]) for i, (s, d) in enumerate(jobs)]
    for copy in copies:
        copy.start()
    for copy in copies:
        copy.wait()


def split_grad_kernel(info, grad, give, keep, sem):
    y = info[2]
    half = grad.shape[1] // 2
    copies = [
        pltpu.make_async_copy(grad.at[:, lanes((1 - y) * half, half)], give, sem.at[0]),
        pltpu.make_async_copy(grad.at[:, lanes(y * half, half)], keep, sem.at[1]),
    ]
    for copy in copies:
        copy.start()
    for copy in copies:
        copy.wait()


def split_heads_kernel(info, q, o, k, v, qo_give, qo_keep, kv_give, kv_keep, sem):
    c = info[1]
    copies = []
    for qo, kv, parity in ((qo_give, kv_give, 1 - c), (qo_keep, kv_keep, c)):
        for slot in range(4):
            head = 2 * slot + parity
            for i, (source, to, width) in enumerate(
                ((q, qo, 256), (o, qo, 256), (k, kv, 128), (v, kv, 128))
            ):
                at = (i % 2) * 4 * width + slot * width
                copies.append(
                    pltpu.make_async_copy(
                        source.at[:, lanes(head * width, width)],
                        to.at[:, at : at + width],
                        sem.at[len(copies)],
                    )
                )
    for copy in copies:
        copy.start()
    for copy in copies:
        copy.wait()


def pick_kernel(info, own, got, base, head):
    base[...] = jnp.where(info[1] == info[2], own[...], got[...])
    head[...] = base[:, : head.shape[1]]


def head_part_kernel(info, give_own, give_other, keep_own, keep_other, mine, other, give, keep):
    x, c = info[0], info[1]
    rows = give_own.shape[0]
    rest_cols = other.shape[1]
    shared = SHARED_COLS
    rest = jnp.concatenate([mine[:, :rest_cols], other[...]], axis=0)
    first = mine[:, rest_cols : rest_cols + shared]
    second = mine[:, rest_cols + shared :]
    common = jnp.concatenate(
        [jnp.where(x == 0, first, second), jnp.where(x == 0, second, first)], axis=0
    )
    for grad, block, out in (
        (give_own, c, give),
        (give_other, 1 - c, give),
        (keep_own, c, keep),
        (keep_other, 1 - c, keep),
    ):
        total = nt(grad[:, shared:], rest) + nt(grad[:, :shared], common)
        out[pl.ds(pl.multiple_of(block * rows, rows), rows), :] = total.astype(out.dtype)


def in_order(c, mine, other):
    first = jnp.where(c == 0, mine, other)
    second = jnp.where(c == 0, other, mine)
    return first, second


def col_max(a):
    return jnp.max(a, axis=0, keepdims=True)


def col_sum(a):
    return jnp.sum(a, axis=0, keepdims=True)


def probs_kernel(info, qo, qo_got, kv, kv_got, far, far_got, pd, px):
    x, c = info[0], info[1]
    b = qo.shape[0]
    scale = score_scale
    key = lax.broadcasted_iota(jnp.int32, (b, b), 0)
    token = lax.broadcasted_iota(jnp.int32, (b, b), 1)
    seen = key <= token

    for slot in range(4):
        at = slot * HEAD_DIM
        key0, key1 = in_order(c, kv[:, at : at + HEAD_DIM], kv_got[:, at : at + HEAD_DIM])
        for head in range(2):
            at = slot * 256 + head * HEAD_DIM
            q0, q1 = in_order(c, qo[:, at : at + HEAD_DIM], qo_got[:, at : at + HEAD_DIM])
            s00 = jnp.where(seen, nt(key0, q0) * scale, masked_value)
            s01 = nt(key0, q1) * scale
            s11 = jnp.where(seen, nt(key1, q1) * scale, masked_value)
            m0 = col_max(s00)
            m1 = jnp.maximum(col_max(s01), col_max(s11))

            def store(m0, m1, more0, more1, inverse):
                e00 = jnp.exp(s00 - m0)
                e01 = jnp.exp(s01 - m1)
                e11 = jnp.exp(s11 - m1)
                i0 = 1.0 / (col_sum(e00) + more0)
                i1 = 1.0 / (col_sum(e01) + col_sum(e11) + more1)
                pd[slot, head, 0:b, 0:b] = (e00 * i0).astype(BF)
                pd[slot, head, 0:b, b:] = (e01 * i1).astype(BF)
                pd[slot, head, b:, b:] = (e11 * i1).astype(BF)
                inverse(i0, i1)

            @pl.when(x == 0)
            def _():
                store(m0, m1, 0.0, 0.0, lambda i0, i1: None)

            @pl.when(x == 1)
            def _():
                at = slot * HEAD_DIM
                f0, f1 = in_order(c, far[:, at : at + HEAD_DIM], far_got[:, at : at + HEAD_DIM])
                t0 = [nt(f, q0) * scale for f in (f0, f1)]
                t1 = [nt(f, q1) * scale for f in (f0, f1)]
                n0 = jnp.maximum(m0, jnp.maximum(col_max(t0[0]), col_max(t0[1])))
                n1 = jnp.maximum(m1, jnp.maximum(col_max(t1[0]), col_max(t1[1])))
                g0 = [jnp.exp(t - n0) for t in t0]
                g1 = [jnp.exp(t - n1) for t in t1]

                def far_store(i0, i1):
                    for i in range(2):
                        px[slot, head, i * b : (i + 1) * b, 0:b] = (g0[i] * i0).astype(BF)
                        px[slot, head, i * b : (i + 1) * b, b:] = (g1[i] * i1).astype(BF)

                store(
                    n0,
                    n1,
                    col_sum(g0[0]) + col_sum(g0[1]),
                    col_sum(g1[0]) + col_sum(g1[1]),
                    far_store,
                )


def grads_kernel(
    info, own, back, qo, qo_got, kv, kv_got, far_kv, far_got, pd, px, dq, near, far, *, step
):
    x, c = info[0], info[1]
    slot = info[3] ^ step
    b = qo.shape[0]
    scale = score_scale
    key_at = lanes(slot * HEAD_DIM, HEAD_DIM)
    value_at = lanes(4 * HEAD_DIM + slot * HEAD_DIM, HEAD_DIM)
    key0, key1 = in_order(c, kv[:, key_at], kv_got[:, key_at])
    value0, value1 = in_order(c, kv[:, value_at], kv_got[:, value_at])
    for i in range(2):
        head = i ^ x
        here = slice(i * HEAD_DIM, (i + 1) * HEAD_DIM)
        q_at = lanes(slot * 256 + head * HEAD_DIM, HEAD_DIM)
        out_at = lanes(1024 + slot * 256 + head * HEAD_DIM, HEAD_DIM)
        head_grad = (own[:, here] + back[:, here].astype(F32)).astype(BF)
        query = jnp.concatenate(in_order(c, qo[:, q_at], qo_got[:, q_at]), axis=0)
        out = jnp.concatenate(in_order(c, qo[:, out_at], qo_got[:, out_at]), axis=0)
        product = head_grad.astype(F32) * out.astype(F32)
        delta = col_sum(jnp.transpose(product)).astype(BF).astype(F32)
        p0 = pd[slot, head, 0:b, :]
        p1 = pd[slot, head, b:, b:]
        d0 = (p0.astype(F32) * (nt(value0, head_grad) - delta)).astype(BF)
        d1 = (p1.astype(F32) * (nt(value1, head_grad[b:]) - delta[:, b:])).astype(BF)
        parts = (
            (slice(0, b), nn(d0, query), nn(p0, head_grad)),
            (slice(b, 2 * b), nn(d1, query[b:]), nn(p1, head_grad[b:])),
        )
        for at, dkey, dvalue in parts:
            if i == 0:
                near[at, :HEAD_DIM] = dkey
                near[at, HEAD_DIM:] = dvalue
            else:
                near[at, :HEAD_DIM] = (near[at, :HEAD_DIM] + dkey) * scale
                near[at, HEAD_DIM:] += dvalue
        dq0 = tn(d0, key0)
        dq1 = dq0[b:] + tn(d1, key1)
        to = lanes(head * HEAD_DIM, HEAD_DIM)

        @pl.when(x == 0)
        def _():
            dq[0:b, to] = (dq0[:b] * scale).astype(BF)
            dq[b:, to] = (dq1 * scale).astype(BF)

        @pl.when(x == 1)
        def _():
            far_key = jnp.concatenate(in_order(c, far_kv[:, key_at], far_got[:, key_at]), axis=0)
            far_value = jnp.concatenate(
                in_order(c, far_kv[:, value_at], far_got[:, value_at]), axis=0
            )
            pf = px[slot, head]
            df = (pf.astype(F32) * (nt(far_value, head_grad) - delta)).astype(BF)
            dqf = tn(df, far_key)
            dq[0:b, to] = ((dq0[:b] + dqf[:b]) * scale).astype(BF)
            dq[b:, to] = ((dq1 + dqf[b:]) * scale).astype(BF)
            dkey = nn(df, query)
            dvalue = nn(pf, head_grad)
            if i == 0:
                far[:, :HEAD_DIM] = dkey
                far[:, HEAD_DIM:] = dvalue
            else:
                far[:, :HEAD_DIM] = (far[:, :HEAD_DIM] + dkey) * scale
                far[:, HEAD_DIM:] += dvalue


def grads_and_round_kernel(*refs, step):
    *rest, far_low, far = refs
    grads_kernel(*rest, far, step=step)

    @pl.when(refs[0][0] == 1)
    def _():
        far_low[...] = far[...].astype(BF)


def merge_kernel(info, dq, near, from_far, mine, crossed):
    c = info[1]
    b = mine.shape[0]
    here = pl.ds(pl.multiple_of(c * b, b), b)
    there = pl.ds(pl.multiple_of((1 - c) * b, b), b)
    for at, out in ((here, mine), (there, crossed)):
        out[:, :256] = dq[at, :]
        out[:, 256:] = (near[at, :] + from_far[at, :].astype(F32)).astype(BF)


def finish_kernel(info, *refs):
    query_out, key_out, value_out = refs[-3:]
    parts = refs[:-3]
    c, z = info[1], info[3]
    for r in range(len(parts) // 2):
        slot = z ^ r
        for part, parity in ((parts[2 * r], c), (parts[2 * r + 1], 1 - c)):
            head = 2 * slot + parity
            query_out[:, lanes(head * 256, 256)] = part[:, :256]
            key_out[:, lanes(head * HEAD_DIM, HEAD_DIM)] = part[:, 256 : 256 + HEAD_DIM]
            value_out[:, lanes(head * HEAD_DIM, HEAD_DIM)] = part[:, 256 + HEAD_DIM :]


def fast_body(queries, projected_keys, projected_values, attention_result, output_grad, out_weight):
    q, k, v, o, og = (
        a[0]
        for a in (queries, projected_keys, projected_values, attention_result, output_grad)
    )
    rows = q.shape[0]
    half = og.shape[1] // 2
    shared = SHARED_COLS
    rest = half - shared
    dp = lax.axis_index("dp")
    ctx = lax.axis_index("ctx")
    z, y = dp // 2, dp % 2
    x, c = ctx // 2, ctx % 2
    info = jnp.stack([x, c, y, z]).astype(jnp.int32)
    dma = pltpu.SemaphoreType.DMA

    piece = ((128, half + shared), BF)
    cross, own_piece = near_call(
        split_weights_kernel, info, [out_weight], [piece, piece], 8,
        in_hbm=True, scratch=[dma((6,))],
    )
    got = send(cross, lambda x, c, y, z: (x, c, 1 - y, z) if y == c else None)

    half_grad = ((rows, half), BF)
    og_give, og_keep = near_call(
        split_grad_kernel, info, [og], [half_grad, half_grad], 8,
        in_hbm=True, scratch=[dma((2,))],
    )
    qo_give, qo_keep, kv_give, kv_keep = near_call(
        split_heads_kernel, info, [q, o, k, v],
        [((rows, 2048), BF)] * 2 + [((rows, 1024), BF)] * 2, 8,
        in_hbm=True, scratch=[dma((32,))],
    )
    forward = lambda x, c, y, z: (1, c, y, z) if x == 0 else None
    forward_other = lambda x, c, y, z: (1, 1 - c, y, z) if x == 0 else None
    backward = lambda x, c, y, z: (0, c, y, z) if x == 1 else None
    far_kv = send(kv_keep, forward)
    far_got = send(kv_give, forward_other)
    kv_got = send(kv_give, over_core)
    qo_got = send(qo_give, over_core)
    keep_core = send(og_keep, over_core)
    give_back = send(og_give, over_y)
    give_core = send(give_back, over_core)

    base, base_head = near_call(pick_kernel, info, [own_piece, got], [piece, ((128, rest), BF)], 8)
    z1 = send(base, over_z(1))
    z2 = send(base, over_z(2))
    z3 = send(z2, over_z(1))
    mine = [base, z1, z2, z3]

    pair = ((4, 2, 2 * rows, 2 * rows), BF)
    pd, px = near_call(
        probs_kernel, info, [qo_keep, qo_got, kv_keep, kv_got, far_kv, far_got],
        [pair, pair], 16,
    )

    finals = []
    for r in range(4):
        other = send(base_head if r == 0 else mine[r][:, :rest], over_x)
        give, keep = near_call(
            head_part_kernel, info,
            [give_back, give_core, og_keep, keep_core, mine[r], other],
            [((2 * rows, 256), BF), ((2 * rows, 256), F32)], 16,
        )
        back = send(give, over_y)
        dq, near, far = near_call(
            functools.partial(grads_and_round_kernel, step=r), info,
            [keep, back, qo_keep, qo_got, kv_keep, kv_got, far_kv, far_got, pd, px],
            [((2 * rows, 256), BF), ((2 * rows, 256), F32), ((2 * rows, 256), BF)], 16,
            scratch=[pltpu.VMEM((2 * rows, 256), F32)],
        )
        from_far = send(far, backward)
        ours, crossed = near_call(
            merge_kernel, info, [dq, near, from_far], [((rows, 512), BF)] * 2, 8
        )
        finals += [ours, send(crossed, over_core)]

    outs = near_call(
        finish_kernel, info, finals, [(a.shape, BF) for a in (q, k, v)], 16, out_hbm=True
    )
    return tuple(a[None] for a in outs)


def fits_fast(mesh):
    return dict(mesh.shape) == {"dp": 8, "ctx": 4}


def chosen_body(mesh):
    def run(queries, projected_keys, projected_values, attention_result, output_grad, out_weight):
        fast = (
            fits_fast(mesh)
            and queries.shape == (1, 256, 2048)
            and out_weight.shape[0] == 256
            and projected_keys.shape == (1, 256, 1024)
            and output_grad.shape[2] % 256 == 0
            and output_grad.shape[2] // 2 > SHARED_COLS
        )
        use = fast_body if fast else body
        return use(
            queries, projected_keys, projected_values, attention_result, output_grad, out_weight
        )

    return run


def solution(mesh):
    placed = (
        P("dp", "ctx", None),
        P("dp", "ctx", None),
        P("dp", "ctx", None),
        P("dp", "ctx", None),
        P("dp", "ctx", None),
        P("dp", None),
    )
    return jax.shard_map(
        chosen_body(mesh),
        mesh=mesh,
        in_specs=placed,
        out_specs=(P("dp", "ctx", None), P("dp", "ctx", None), P("dp", "ctx", None)),
        check_vma=False,
    )
```

```python
import functools

import jax
import jax.numpy as jnp
from jax import lax
from jax.experimental import pallas as pl
from jax.experimental.pallas import tpu as pltpu
from jax.sharding import PartitionSpec as P


KEY_HEAD_COUNT = 8
HEAD_DIM = 128
WINDOW = 1024


score_scale = 168.0 ** (-0.5)
masked_value = -1e30


def band_backward(
    query_head_total, key_head_total, value_head_total, gradient_by_head, delta_heads
):
    sequence_tokens, local_kv, query_feature_width = query_head_total.shape
    head_size = key_head_total.shape[2]
    queries_per_group = query_feature_width // head_size
    block_rows = min(512, sequence_tokens)
    span_len = WINDOW + block_rows
    query_four = query_head_total.reshape(sequence_tokens, local_kv, queries_per_group, head_size)
    gradient_rank_four = gradient_by_head.reshape(
        sequence_tokens, local_kv, queries_per_group, head_size
    )
    leading = jnp.zeros((WINDOW, local_kv, head_size), key_head_total.dtype)
    key_padded = jnp.concatenate([leading, key_head_total], axis=0)
    value_padded = jnp.concatenate([leading, value_head_total], axis=0)
    delta_float = delta_heads.astype(jnp.float32)

    def one_block(block_index, totals):
        query_total, key_total, value_total = totals
        first_row = (block_index * block_rows).astype(jnp.int32)
        query_block = lax.dynamic_slice_in_dim(query_four, first_row, block_rows, 0)
        grad_block = lax.dynamic_slice_in_dim(gradient_rank_four, first_row, block_rows, 0)
        delta_block = lax.dynamic_slice_in_dim(delta_float, first_row, block_rows, 0)
        key_block = lax.dynamic_slice_in_dim(key_padded, first_row, span_len, 0)
        value_block = lax.dynamic_slice_in_dim(value_padded, first_row, span_len, 0)
        scores = (
            jnp.einsum("qhgd,khd->hgqk", query_block, key_block, preferred_element_type=jnp.float32)
            * score_scale
        )
        query_pos = first_row + lax.iota(jnp.int32, block_rows)
        key_pos = first_row - WINDOW + lax.iota(jnp.int32, span_len)
        visible = (
            (key_pos[None, :] <= query_pos[:, None])
            & (key_pos[None, :] > query_pos[:, None] - WINDOW)
            & (key_pos[None, :] >= 0)
        )
        scores = jnp.where(visible, scores, masked_value)
        highest = jnp.max(scores, axis=-1, keepdims=True)
        expos = jnp.exp(scores - highest)
        probs = expos / jnp.sum(expos, axis=-1, keepdims=True)
        probs_low = probs.astype(jnp.bfloat16)
        dprobs = jnp.einsum(
            "qhgd,khd->hgqk", grad_block, value_block, preferred_element_type=jnp.float32
        )
        delta_rows = jnp.transpose(delta_block, (1, 2, 0))[..., None]
        dscores = (probs * (dprobs - delta_rows)).astype(jnp.bfloat16)
        query_part = (
            jnp.einsum("hgqk,khd->qhgd", dscores, key_block, preferred_element_type=jnp.float32)
            * score_scale
        )
        key_portion = (
            jnp.einsum("hgqk,qhgd->khd", dscores, query_block, preferred_element_type=jnp.float32)
            * score_scale
        )
        value_portion = jnp.einsum(
            "hgqk,qhgd->khd", probs_low, grad_block, preferred_element_type=jnp.float32
        )
        query_total = lax.dynamic_update_slice_in_dim(
            query_total, query_part.reshape(block_rows, local_kv, query_feature_width), first_row, 0
        )
        key_total = lax.dynamic_update_slice_in_dim(
            key_total,
            lax.dynamic_slice_in_dim(key_total, first_row, span_len, 0) + key_portion,
            first_row,
            0,
        )
        value_total = lax.dynamic_update_slice_in_dim(
            value_total,
            lax.dynamic_slice_in_dim(value_total, first_row, span_len, 0) + value_portion,
            first_row,
            0,
        )
        return (query_total, key_total, value_total)

    initial = (
        jnp.zeros((sequence_tokens, local_kv, query_feature_width), jnp.float32),
        jnp.zeros((WINDOW + sequence_tokens, local_kv, head_size), jnp.float32),
        jnp.zeros((WINDOW + sequence_tokens, local_kv, head_size), jnp.float32),
    )
    query_total, key_total, value_total = lax.fori_loop(
        0, sequence_tokens // block_rows, one_block, initial
    )
    return (
        query_total.astype(jnp.bfloat16),
        key_total[WINDOW:].astype(jnp.bfloat16),
        value_total[WINDOW:].astype(jnp.bfloat16),
    )


def head_delta(gradient_rank_three, output_rank_three):
    rows_here, heads_here, query_feature_width = gradient_rank_three.shape
    queries_per_group = query_feature_width // HEAD_DIM
    gradient_rank_four = gradient_rank_three.reshape(
        rows_here, heads_here, queries_per_group, HEAD_DIM
    ).astype(jnp.float32)
    output_rank_four = output_rank_three.reshape(
        rows_here, heads_here, queries_per_group, HEAD_DIM
    ).astype(jnp.float32)
    return jnp.sum(gradient_rank_four * output_rank_four, axis=-1).astype(jnp.bfloat16)


def one_sequence(query_rows, key_rows, value_rows, output_rows, gradient_rows):
    token_total = query_rows.shape[0]
    query_feature_width = query_rows.shape[1]
    queries_per_group = query_feature_width // (KEY_HEAD_COUNT * HEAD_DIM)
    query_rank_three = query_rows.reshape(token_total, KEY_HEAD_COUNT, queries_per_group * HEAD_DIM)
    key_rank_three = key_rows.reshape(token_total, KEY_HEAD_COUNT, HEAD_DIM)
    value_rank_three = value_rows.reshape(token_total, KEY_HEAD_COUNT, HEAD_DIM)
    output_rank_three = output_rows.reshape(
        token_total, KEY_HEAD_COUNT, queries_per_group * HEAD_DIM
    )
    gradient_rank_three = gradient_rows.reshape(
        token_total, KEY_HEAD_COUNT, queries_per_group * HEAD_DIM
    )
    query_head_total, key_head_total, value_head_total, output_heads = (
        lax.all_to_all(query_rank_three, "ctx", split_axis=1, concat_axis=0, tiled=True),
        lax.all_to_all(key_rank_three, "ctx", split_axis=1, concat_axis=0, tiled=True),
        lax.all_to_all(value_rank_three, "ctx", split_axis=1, concat_axis=0, tiled=True),
        lax.all_to_all(output_rank_three, "ctx", split_axis=1, concat_axis=0, tiled=True),
    )
    gradient_by_head = lax.all_to_all(
        gradient_rank_three, "ctx", split_axis=1, concat_axis=0, tiled=True
    )
    delta_heads = head_delta(gradient_by_head, output_heads)
    query_back, key_back, value_back = band_backward(
        query_head_total, key_head_total, value_head_total, gradient_by_head, delta_heads
    )
    query_local, key_slice_here, value_slice_here = (
        lax.all_to_all(query_back, "ctx", split_axis=0, concat_axis=1, tiled=True),
        lax.all_to_all(key_back, "ctx", split_axis=0, concat_axis=1, tiled=True),
        lax.all_to_all(value_back, "ctx", split_axis=0, concat_axis=1, tiled=True),
    )
    return (
        query_local.reshape(token_total, query_feature_width),
        key_slice_here.reshape(token_total, KEY_HEAD_COUNT * HEAD_DIM),
        value_slice_here.reshape(token_total, KEY_HEAD_COUNT * HEAD_DIM),
    )


def body(queries, projected_keys, projected_values, attention_result, output_grad, out_weight):
    sequences_here = queries.shape[0]
    token_total = queries.shape[1]
    query_feature_width = queries.shape[2]
    row_total = sequences_here * token_total
    grad_rows = output_grad.reshape(row_total, output_grad.shape[2])
    per_head_gradient = lax.dot_general(
        grad_rows,
        lax.all_gather(out_weight, "dp", axis=0, tiled=True),
        (((1,), (1,)), ((), ())),
        preferred_element_type=jnp.float32,
    ).astype(jnp.bfloat16)
    per_head_gradient = per_head_gradient.reshape(sequences_here, token_total, query_feature_width)
    query_part, key_part, value_part = one_sequence(
        queries[0],
        projected_keys[0],
        projected_values[0],
        attention_result[0],
        per_head_gradient[0],
    )
    query_list = [query_part]
    key_list = [key_part]
    value_list = [value_part]
    return (
        jnp.stack(query_list, axis=0),
        jnp.stack(key_list, axis=0),
        jnp.stack(value_list, axis=0),
    )


AXES = ("dp", "ctx")
SHARED_COLS = 640
BF = jnp.bfloat16
F32 = jnp.float32


def place(x, c, y, z):
    return (z * 2 + y) * 4 + x * 2 + c


def pairs(target):
    found = []
    for z in range(4):
        for y in range(2):
            for x in range(2):
                for c in range(2):
                    to = target(x, c, y, z)
                    if to is not None:
                        found.append((place(x, c, y, z), place(*to)))
    return found


def send(value, target):
    return lax.ppermute(value, AXES, pairs(target))


def over_x(x, c, y, z):
    return (1 - x, c, y, z)


def over_y(x, c, y, z):
    return (x, c, 1 - y, z)


def over_core(x, c, y, z):
    return (x, 1 - c, y, z)


def over_z(step):
    return lambda x, c, y, z: (x, c, y, z ^ step)


def nt(a, b):
    return lax.dot_general(a, b, (((1,), (1,)), ((), ())), preferred_element_type=F32)


def nn(a, b):
    return lax.dot_general(a, b, (((1,), (0,)), ((), ())), preferred_element_type=F32)


def tn(a, b):
    return lax.dot_general(a, b, (((0,), (0,)), ((), ())), preferred_element_type=F32)


def near_call(kernel, info, args, outs, limit, in_hbm=False, out_hbm=False, scratch=()):
    vmem = pl.BlockSpec(memory_space=pltpu.VMEM)
    wide = pl.BlockSpec(memory_space=pltpu.HBM)
    space = pltpu.HBM if in_hbm else pltpu.VMEM
    args = [pltpu.with_memory_space_constraint(a, space) for a in args]
    shapes = [
        jax.ShapeDtypeStruct(s, d) if out_hbm else pltpu.VMEM(s, d) for s, d in outs
    ]
    return pl.pallas_call(
        kernel,
        in_specs=[pl.BlockSpec(memory_space=pltpu.SMEM)]
        + [wide if in_hbm else vmem] * len(args),
        out_specs=[vmem] * len(outs),
        out_shape=shapes,
        scratch_shapes=list(scratch),
        compiler_params=pltpu.CompilerParams(vmem_limit_bytes=limit * 1024 * 1024),
    )(info, *args)


def lanes(start, size):
    return pl.ds(pl.multiple_of(start, HEAD_DIM), size)


def split_weights_kernel(info, weight, cross_rest, cross_both, own_rest, own_both, sem):
    x, y = info[0], info[2]
    half = weight.shape[1] // 2
    shared = SHARED_COLS
    rest = half - shared
    copies = []
    for to_rest, to_both, side in ((cross_rest, cross_both, 1 - y), (own_rest, own_both, y)):
        first = side * half
        for source, to in (
            (weight.at[lanes(x * 128, 128), lanes(first + shared, rest)], to_rest),
            (weight.at[0:128, lanes(first, shared)], to_both.at[:, :shared]),
            (weight.at[128:256, lanes(first, shared)], to_both.at[:, shared:]),
        ):
            copies.append(pltpu.make_async_copy(source, to, sem.at[len(copies)]))
    for copy in copies:
        copy.start()
    for copy in copies:
        copy.wait()


def split_grad_kernel(info, grad, give, keep, sem):
    y = info[2]
    half = grad.shape[1] // 2
    copies = [
        pltpu.make_async_copy(grad.at[:, lanes((1 - y) * half, half)], give, sem.at[0]),
        pltpu.make_async_copy(grad.at[:, lanes(y * half, half)], keep, sem.at[1]),
    ]
    for copy in copies:
        copy.start()
    for copy in copies:
        copy.wait()


def split_heads_kernel(info, q, o, k, v, qo_give, qo_keep, kv_give, kv_keep, sem):
    c = info[1]
    copies = []
    for qo, kv, parity in ((qo_give, kv_give, 1 - c), (qo_keep, kv_keep, c)):
        for slot in range(4):
            head = 2 * slot + parity
            for i, (source, to, width) in enumerate(
                ((q, qo, 256), (o, qo, 256), (k, kv, 128), (v, kv, 128))
            ):
                at = (i % 2) * 4 * width + slot * width
                copies.append(
                    pltpu.make_async_copy(
                        source.at[:, lanes(head * width, width)],
                        to.at[:, at : at + width],
                        sem.at[len(copies)],
                    )
                )
    for copy in copies:
        copy.start()
    for copy in copies:
        copy.wait()


def pick_kernel(info, own, got, out):
    out[...] = jnp.where(info[1] == info[2], own[...], got[...])


def head_part_kernel(info, give_own, give_other, keep_own, keep_other, both, *refs, which):
    x, c = info[0], info[1]
    rows = give_own.shape[0]
    shared = SHARED_COLS
    weights = refs[: len(which)]
    give, keep = refs[len(which) :]
    first = both[:, :shared]
    second = both[:, shared:]
    common = [
        jnp.where(x == 0, first, second) if i == 0 else jnp.where(x == 0, second, first)
        for i in which
    ]
    rest = [w[...] for w in weights]
    if len(which) == 2:
        common = [jnp.concatenate(common, axis=0)]
        rest = [jnp.concatenate(rest, axis=0)]
    for grad, block, out in (
        (give_own, c, give),
        (give_other, 1 - c, give),
        (keep_own, c, keep),
        (keep_other, 1 - c, keep),
    ):
        total = nt(grad[:, shared:], rest[0]) + nt(grad[:, :shared], common[0])
        out[pl.ds(pl.multiple_of(block * rows, rows), rows), :] = total.astype(out.dtype)


def in_order(c, mine, other):
    first = jnp.where(c == 0, mine, other)
    second = jnp.where(c == 0, other, mine)
    return first, second


def col_max(a):
    return jnp.max(a, axis=0, keepdims=True)


def col_sum(a):
    return jnp.sum(a, axis=0, keepdims=True)


def probs_kernel(info, qo, qo_got, kv, kv_got, far, far_got, pd, px):
    x, c = info[0], info[1]
    b = qo.shape[0]
    scale = score_scale
    key = lax.broadcasted_iota(jnp.int32, (b, b), 0)
    token = lax.broadcasted_iota(jnp.int32, (b, b), 1)
    seen = key <= token

    for slot in range(4):
        at = slot * HEAD_DIM
        key0, key1 = in_order(c, kv[:, at : at + HEAD_DIM], kv_got[:, at : at + HEAD_DIM])
        for head in range(2):
            at = slot * 256 + head * HEAD_DIM
            q0, q1 = in_order(c, qo[:, at : at + HEAD_DIM], qo_got[:, at : at + HEAD_DIM])
            s00 = jnp.where(seen, nt(key0, q0) * scale, masked_value)
            s01 = nt(key0, q1) * scale
            s11 = jnp.where(seen, nt(key1, q1) * scale, masked_value)
            m0 = col_max(s00)
            m1 = jnp.maximum(col_max(s01), col_max(s11))

            def store(m0, m1, more0, more1, inverse):
                e00 = jnp.exp(s00 - m0)
                e01 = jnp.exp(s01 - m1)
                e11 = jnp.exp(s11 - m1)
                i0 = 1.0 / (col_sum(e00) + more0)
                i1 = 1.0 / (col_sum(e01) + col_sum(e11) + more1)
                pd[slot, head, 0:b, 0:b] = (e00 * i0).astype(BF)
                pd[slot, head, 0:b, b:] = (e01 * i1).astype(BF)
                pd[slot, head, b:, b:] = (e11 * i1).astype(BF)
                inverse(i0, i1)

            @pl.when(x == 0)
            def _():
                store(m0, m1, 0.0, 0.0, lambda i0, i1: None)

            @pl.when(x == 1)
            def _():
                at = slot * HEAD_DIM
                f0, f1 = in_order(c, far[:, at : at + HEAD_DIM], far_got[:, at : at + HEAD_DIM])
                t0 = [nt(f, q0) * scale for f in (f0, f1)]
                t1 = [nt(f, q1) * scale for f in (f0, f1)]
                n0 = jnp.maximum(m0, jnp.maximum(col_max(t0[0]), col_max(t0[1])))
                n1 = jnp.maximum(m1, jnp.maximum(col_max(t1[0]), col_max(t1[1])))
                g0 = [jnp.exp(t - n0) for t in t0]
                g1 = [jnp.exp(t - n1) for t in t1]

                def far_store(i0, i1):
                    for i in range(2):
                        px[slot, head, i * b : (i + 1) * b, 0:b] = (g0[i] * i0).astype(BF)
                        px[slot, head, i * b : (i + 1) * b, b:] = (g1[i] * i1).astype(BF)

                store(
                    n0,
                    n1,
                    col_sum(g0[0]) + col_sum(g0[1]),
                    col_sum(g1[0]) + col_sum(g1[1]),
                    far_store,
                )


def grads_kernel(info, own, back, qo, qo_got, kv, kv_got, far_kv, far_got, pd, px, *refs, step, which):
    x, c = info[0], info[1]
    slot = info[3] ^ step
    last = 1 in which
    carried = last and 0 not in which
    if carried:
        near_in, far_in, *refs = refs
    if last:
        dq, near, far_low, far = refs
    else:
        dq, near, far = refs
    b = qo.shape[0]
    scale = score_scale
    key_at = lanes(slot * HEAD_DIM, HEAD_DIM)
    value_at = lanes(4 * HEAD_DIM + slot * HEAD_DIM, HEAD_DIM)
    key0, key1 = in_order(c, kv[:, key_at], kv_got[:, key_at])
    value0, value1 = in_order(c, kv[:, value_at], kv_got[:, value_at])

    def put(to, at, dkey, dvalue, i):
        if i == 1:
            source = near_in if carried and to is near else far_in if carried else to
            dkey = (source[at, :HEAD_DIM] + dkey) * scale
            dvalue = source[at, HEAD_DIM:] + dvalue
        to[at, :HEAD_DIM] = dkey
        to[at, HEAD_DIM:] = dvalue

    for place_in, i in enumerate(which):
        head = i ^ x
        here = slice(place_in * HEAD_DIM, (place_in + 1) * HEAD_DIM)
        q_at = lanes(slot * 256 + head * HEAD_DIM, HEAD_DIM)
        out_at = lanes(1024 + slot * 256 + head * HEAD_DIM, HEAD_DIM)
        head_grad = (own[:, here] + back[:, here].astype(F32)).astype(BF)
        query = jnp.concatenate(in_order(c, qo[:, q_at], qo_got[:, q_at]), axis=0)
        out = jnp.concatenate(in_order(c, qo[:, out_at], qo_got[:, out_at]), axis=0)
        product = head_grad.astype(F32) * out.astype(F32)
        delta = col_sum(jnp.transpose(product)).astype(BF).astype(F32)
        p0 = pd[slot, head, 0:b, :]
        p1 = pd[slot, head, b:, b:]
        d0 = (p0.astype(F32) * (nt(value0, head_grad) - delta)).astype(BF)
        d1 = (p1.astype(F32) * (nt(value1, head_grad[b:]) - delta[:, b:])).astype(BF)
        put(near, slice(0, b), nn(d0, query), nn(p0, head_grad), i)
        put(near, slice(b, 2 * b), nn(d1, query[b:]), nn(p1, head_grad[b:]), i)
        dq0 = tn(d0, key0)
        dq1 = dq0[b:] + tn(d1, key1)
        to = lanes(head * HEAD_DIM, HEAD_DIM) if len(which) == 2 else slice(0, HEAD_DIM)

        @pl.when(x == 0)
        def _():
            dq[0:b, to] = (dq0[:b] * scale).astype(BF)
            dq[b:, to] = (dq1 * scale).astype(BF)

        @pl.when(x == 1)
        def _():
            far_key = jnp.concatenate(in_order(c, far_kv[:, key_at], far_got[:, key_at]), axis=0)
            far_value = jnp.concatenate(
                in_order(c, far_kv[:, value_at], far_got[:, value_at]), axis=0
            )
            pf = px[slot, head]
            df = (pf.astype(F32) * (nt(far_value, head_grad) - delta)).astype(BF)
            dqf = tn(df, far_key)
            dq[0:b, to] = ((dq0[:b] + dqf[:b]) * scale).astype(BF)
            dq[b:, to] = ((dq1 + dqf[b:]) * scale).astype(BF)
            put(far, slice(0, 2 * b), nn(df, query), nn(pf, head_grad), i)

    if last:

        @pl.when(x == 1)
        def _():
            far_low[...] = far[...].astype(BF)


def merge_kernel(info, *refs):
    *dqs, near, from_far, mine, crossed = refs
    x, c = info[0], info[1]
    b = mine.shape[0]
    here = pl.ds(pl.multiple_of(c * b, b), b)
    there = pl.ds(pl.multiple_of((1 - c) * b, b), b)
    for at, out in ((here, mine), (there, crossed)):
        if len(dqs) == 1:
            out[:, :256] = dqs[0][at, :]
        else:
            for i, dq in enumerate(dqs):
                out[:, lanes((i ^ x) * HEAD_DIM, HEAD_DIM)] = dq[at, :]
        more = jnp.where(x == 0, from_far[at, :].astype(F32), 0.0)
        out[:, 256:] = (near[at, :] + more).astype(BF)


def finish_kernel(info, *refs):
    query_out, key_out, value_out = refs[-3:]
    parts = refs[:-3]
    c, z = info[1], info[3]
    for r in range(len(parts) // 2):
        slot = z ^ r
        for part, parity in ((parts[2 * r], c), (parts[2 * r + 1], 1 - c)):
            head = 2 * slot + parity
            query_out[:, lanes(head * 256, 256)] = part[:, :256]
            key_out[:, lanes(head * HEAD_DIM, HEAD_DIM)] = part[:, 256 : 256 + HEAD_DIM]
            value_out[:, lanes(head * HEAD_DIM, HEAD_DIM)] = part[:, 256 + HEAD_DIM :]


def fast_body(queries, projected_keys, projected_values, attention_result, output_grad, out_weight):
    q, k, v, o, og = (
        a[0]
        for a in (queries, projected_keys, projected_values, attention_result, output_grad)
    )
    rows = q.shape[0]
    half = og.shape[1] // 2
    shared = SHARED_COLS
    rest = half - shared
    dp = lax.axis_index("dp")
    ctx = lax.axis_index("ctx")
    z, y = dp // 2, dp % 2
    x, c = ctx // 2, ctx % 2
    info = jnp.stack([x, c, y, z]).astype(jnp.int32)
    dma = pltpu.SemaphoreType.DMA

    thin = ((128, rest), BF)
    both = ((128, 2 * shared), BF)
    cross_rest, cross_both, own_rest, own_both = near_call(
        split_weights_kernel, info, [out_weight], [thin, both, thin, both], 8,
        in_hbm=True, scratch=[dma((6,))],
    )
    to_other = lambda x, c, y, z: (x, c, 1 - y, z) if y == c else None
    got_rest = send(cross_rest, to_other)
    got_both = send(cross_both, to_other)

    def pick(own, got, shape):
        return near_call(pick_kernel, info, [own, got], [shape], 8)[0]

    half_grad = ((rows, half), BF)
    og_give, og_keep = near_call(
        split_grad_kernel, info, [og], [half_grad, half_grad], 8,
        in_hbm=True, scratch=[dma((2,))],
    )
    qo_give, qo_keep, kv_give, kv_keep = near_call(
        split_heads_kernel, info, [q, o, k, v],
        [((rows, 2048), BF)] * 2 + [((rows, 1024), BF)] * 2, 8,
        in_hbm=True, scratch=[dma((32,))],
    )
    over_x_and_core = lambda x, c, y, z: (1 - x, 1 - c, y, z)
    far_kv = send(kv_keep, over_x)
    far_got = send(kv_give, over_x_and_core)
    kv_got = send(kv_give, over_core)
    qo_got = send(qo_give, over_core)
    keep_core = send(og_keep, over_core)
    give_back = send(og_give, over_y)
    give_core = send(give_back, over_core)

    w_rest = pick(own_rest, got_rest, thin)
    w_both = pick(own_both, got_both, both)
    rests, boths = [w_rest], [w_both]
    for step in (1, 2):
        rests.append(send(w_rest, over_z(step)))
        boths.append(send(w_both, over_z(step)))
    rests.append(send(rests[2], over_z(1)))
    boths.append(send(boths[2], over_z(1)))

    pair = ((4, 2, 2 * rows, 2 * rows), BF)
    pd, px = near_call(
        probs_kernel, info, [qo_keep, qo_got, kv_keep, kv_got, far_kv, far_got],
        [pair, pair], 16,
    )

    def part(r, which, weights):
        width = HEAD_DIM * len(which)
        return near_call(
            functools.partial(head_part_kernel, which=which), info,
            [give_back, give_core, og_keep, keep_core, boths[r]] + weights,
            [((2 * rows, width), BF), ((2 * rows, width), F32)], 16,
        )

    def grads(r, which, keep, back, carry):
        key_sums = ((2 * rows, 256), F32)
        last = 1 in which
        return near_call(
            functools.partial(grads_kernel, step=r, which=which), info,
            [keep, back, qo_keep, qo_got, kv_keep, kv_got, far_kv, far_got, pd, px] + carry,
            [((2 * rows, HEAD_DIM * len(which)), BF), key_sums]
            + [((2 * rows, 256), BF) if last else key_sums], 16,
            scratch=[pltpu.VMEM(*key_sums)] if last else [],
        )

    finals = []
    for r in range(4):
        other = send(rests[r], over_x)
        split = r == 3
        groups = ((0,), (1,)) if split else ((0, 1),)
        carry = []
        dqs = []
        for which in groups:
            weights = [(rests[r], other)[i] for i in which]
            give, keep = part(r, which, weights)
            back = send(give, over_y)
            dq, near, far = grads(r, which, keep, back, carry)
            carry = [near, far]
            dqs.append(dq)
        from_far = send(far, over_x)
        ours, crossed = near_call(
            merge_kernel, info, dqs + [near, from_far], [((rows, 512), BF)] * 2, 8
        )
        finals += [ours, send(crossed, over_core)]

    outs = near_call(
        finish_kernel, info, finals, [(a.shape, BF) for a in (q, k, v)], 16, out_hbm=True
    )
    return tuple(a[None] for a in outs)


def fits_fast(mesh):
    return dict(mesh.shape) == {"dp": 8, "ctx": 4}


def chosen_body(mesh):
    def run(queries, projected_keys, projected_values, attention_result, output_grad, out_weight):
        fast = (
            fits_fast(mesh)
            and queries.shape == (1, 256, 2048)
            and out_weight.shape[0] == 256
            and projected_keys.shape == (1, 256, 1024)
            and output_grad.shape[2] % 256 == 0
            and output_grad.shape[2] // 2 > SHARED_COLS
        )
        use = fast_body if fast else body
        return use(
            queries, projected_keys, projected_values, attention_result, output_grad, out_weight
        )

    return run


def solution(mesh):
    placed = (
        P("dp", "ctx", None),
        P("dp", "ctx", None),
        P("dp", "ctx", None),
        P("dp", "ctx", None),
        P("dp", "ctx", None),
        P("dp", None),
    )
    step = jax.shard_map(
        chosen_body(mesh),
        mesh=mesh,
        in_specs=placed,
        out_specs=(P("dp", "ctx", None), P("dp", "ctx", None), P("dp", "ctx", None)),
        check_vma=False,
    )
    if not fits_fast(mesh):
        return step
    return step
```

```python
import functools

import jax
import jax.numpy as jnp
from jax import lax
from jax.experimental import pallas as pl
from jax.experimental.pallas import tpu as pltpu
from jax.sharding import PartitionSpec as P


KEY_HEAD_COUNT = 8
HEAD_DIM = 128
WINDOW = 1024


score_scale = 168.0 ** (-0.5)
masked_value = -1e30


def band_backward(
    query_head_total, key_head_total, value_head_total, gradient_by_head, delta_heads
):
    sequence_tokens, local_kv, query_feature_width = query_head_total.shape
    head_size = key_head_total.shape[2]
    queries_per_group = query_feature_width // head_size
    block_rows = min(512, sequence_tokens)
    span_len = WINDOW + block_rows
    query_four = query_head_total.reshape(sequence_tokens, local_kv, queries_per_group, head_size)
    gradient_rank_four = gradient_by_head.reshape(
        sequence_tokens, local_kv, queries_per_group, head_size
    )
    leading = jnp.zeros((WINDOW, local_kv, head_size), key_head_total.dtype)
    key_padded = jnp.concatenate([leading, key_head_total], axis=0)
    value_padded = jnp.concatenate([leading, value_head_total], axis=0)
    delta_float = delta_heads.astype(jnp.float32)

    def one_block(block_index, totals):
        query_total, key_total, value_total = totals
        first_row = (block_index * block_rows).astype(jnp.int32)
        query_block = lax.dynamic_slice_in_dim(query_four, first_row, block_rows, 0)
        grad_block = lax.dynamic_slice_in_dim(gradient_rank_four, first_row, block_rows, 0)
        delta_block = lax.dynamic_slice_in_dim(delta_float, first_row, block_rows, 0)
        key_block = lax.dynamic_slice_in_dim(key_padded, first_row, span_len, 0)
        value_block = lax.dynamic_slice_in_dim(value_padded, first_row, span_len, 0)
        scores = (
            jnp.einsum("qhgd,khd->hgqk", query_block, key_block, preferred_element_type=jnp.float32)
            * score_scale
        )
        query_pos = first_row + lax.iota(jnp.int32, block_rows)
        key_pos = first_row - WINDOW + lax.iota(jnp.int32, span_len)
        visible = (
            (key_pos[None, :] <= query_pos[:, None])
            & (key_pos[None, :] > query_pos[:, None] - WINDOW)
            & (key_pos[None, :] >= 0)
        )
        scores = jnp.where(visible, scores, masked_value)
        highest = jnp.max(scores, axis=-1, keepdims=True)
        expos = jnp.exp(scores - highest)
        probs = expos / jnp.sum(expos, axis=-1, keepdims=True)
        probs_low = probs.astype(jnp.bfloat16)
        dprobs = jnp.einsum(
            "qhgd,khd->hgqk", grad_block, value_block, preferred_element_type=jnp.float32
        )
        delta_rows = jnp.transpose(delta_block, (1, 2, 0))[..., None]
        dscores = (probs * (dprobs - delta_rows)).astype(jnp.bfloat16)
        query_part = (
            jnp.einsum("hgqk,khd->qhgd", dscores, key_block, preferred_element_type=jnp.float32)
            * score_scale
        )
        key_portion = (
            jnp.einsum("hgqk,qhgd->khd", dscores, query_block, preferred_element_type=jnp.float32)
            * score_scale
        )
        value_portion = jnp.einsum(
            "hgqk,qhgd->khd", probs_low, grad_block, preferred_element_type=jnp.float32
        )
        query_total = lax.dynamic_update_slice_in_dim(
            query_total, query_part.reshape(block_rows, local_kv, query_feature_width), first_row, 0
        )
        key_total = lax.dynamic_update_slice_in_dim(
            key_total,
            lax.dynamic_slice_in_dim(key_total, first_row, span_len, 0) + key_portion,
            first_row,
            0,
        )
        value_total = lax.dynamic_update_slice_in_dim(
            value_total,
            lax.dynamic_slice_in_dim(value_total, first_row, span_len, 0) + value_portion,
            first_row,
            0,
        )
        return (query_total, key_total, value_total)

    initial = (
        jnp.zeros((sequence_tokens, local_kv, query_feature_width), jnp.float32),
        jnp.zeros((WINDOW + sequence_tokens, local_kv, head_size), jnp.float32),
        jnp.zeros((WINDOW + sequence_tokens, local_kv, head_size), jnp.float32),
    )
    query_total, key_total, value_total = lax.fori_loop(
        0, sequence_tokens // block_rows, one_block, initial
    )
    return (
        query_total.astype(jnp.bfloat16),
        key_total[WINDOW:].astype(jnp.bfloat16),
        value_total[WINDOW:].astype(jnp.bfloat16),
    )


def head_delta(gradient_rank_three, output_rank_three):
    rows_here, heads_here, query_feature_width = gradient_rank_three.shape
    queries_per_group = query_feature_width // HEAD_DIM
    gradient_rank_four = gradient_rank_three.reshape(
        rows_here, heads_here, queries_per_group, HEAD_DIM
    ).astype(jnp.float32)
    output_rank_four = output_rank_three.reshape(
        rows_here, heads_here, queries_per_group, HEAD_DIM
    ).astype(jnp.float32)
    return jnp.sum(gradient_rank_four * output_rank_four, axis=-1).astype(jnp.bfloat16)


def one_sequence(query_rows, key_rows, value_rows, output_rows, gradient_rows):
    token_total = query_rows.shape[0]
    query_feature_width = query_rows.shape[1]
    queries_per_group = query_feature_width // (KEY_HEAD_COUNT * HEAD_DIM)
    query_rank_three = query_rows.reshape(token_total, KEY_HEAD_COUNT, queries_per_group * HEAD_DIM)
    key_rank_three = key_rows.reshape(token_total, KEY_HEAD_COUNT, HEAD_DIM)
    value_rank_three = value_rows.reshape(token_total, KEY_HEAD_COUNT, HEAD_DIM)
    output_rank_three = output_rows.reshape(
        token_total, KEY_HEAD_COUNT, queries_per_group * HEAD_DIM
    )
    gradient_rank_three = gradient_rows.reshape(
        token_total, KEY_HEAD_COUNT, queries_per_group * HEAD_DIM
    )
    query_head_total, key_head_total, value_head_total, output_heads = (
        lax.all_to_all(query_rank_three, "ctx", split_axis=1, concat_axis=0, tiled=True),
        lax.all_to_all(key_rank_three, "ctx", split_axis=1, concat_axis=0, tiled=True),
        lax.all_to_all(value_rank_three, "ctx", split_axis=1, concat_axis=0, tiled=True),
        lax.all_to_all(output_rank_three, "ctx", split_axis=1, concat_axis=0, tiled=True),
    )
    gradient_by_head = lax.all_to_all(
        gradient_rank_three, "ctx", split_axis=1, concat_axis=0, tiled=True
    )
    delta_heads = head_delta(gradient_by_head, output_heads)
    query_back, key_back, value_back = band_backward(
        query_head_total, key_head_total, value_head_total, gradient_by_head, delta_heads
    )
    query_local, key_slice_here, value_slice_here = (
        lax.all_to_all(query_back, "ctx", split_axis=0, concat_axis=1, tiled=True),
        lax.all_to_all(key_back, "ctx", split_axis=0, concat_axis=1, tiled=True),
        lax.all_to_all(value_back, "ctx", split_axis=0, concat_axis=1, tiled=True),
    )
    return (
        query_local.reshape(token_total, query_feature_width),
        key_slice_here.reshape(token_total, KEY_HEAD_COUNT * HEAD_DIM),
        value_slice_here.reshape(token_total, KEY_HEAD_COUNT * HEAD_DIM),
    )


def body(queries, projected_keys, projected_values, attention_result, output_grad, out_weight):
    sequences_here = queries.shape[0]
    token_total = queries.shape[1]
    query_feature_width = queries.shape[2]
    row_total = sequences_here * token_total
    grad_rows = output_grad.reshape(row_total, output_grad.shape[2])
    per_head_gradient = lax.dot_general(
        grad_rows,
        lax.all_gather(out_weight, "dp", axis=0, tiled=True),
        (((1,), (1,)), ((), ())),
        preferred_element_type=jnp.float32,
    ).astype(jnp.bfloat16)
    per_head_gradient = per_head_gradient.reshape(sequences_here, token_total, query_feature_width)
    query_part, key_part, value_part = one_sequence(
        queries[0],
        projected_keys[0],
        projected_values[0],
        attention_result[0],
        per_head_gradient[0],
    )
    query_list = [query_part]
    key_list = [key_part]
    value_list = [value_part]
    return (
        jnp.stack(query_list, axis=0),
        jnp.stack(key_list, axis=0),
        jnp.stack(value_list, axis=0),
    )


AXES = ("dp", "ctx")
SHARED_COLS = 640
PREFETCH = False
EARLY_Z = False
BF = jnp.bfloat16
F32 = jnp.float32


def place(x, c, y, z):
    return (z * 2 + y) * 4 + x * 2 + c


def pairs(target):
    found = []
    for z in range(4):
        for y in range(2):
            for x in range(2):
                for c in range(2):
                    to = target(x, c, y, z)
                    if to is not None:
                        found.append((place(x, c, y, z), place(*to)))
    return found


def send(value, target):
    return lax.ppermute(value, AXES, pairs(target))


def over_x(x, c, y, z):
    return (1 - x, c, y, z)


def over_y(x, c, y, z):
    return (x, c, 1 - y, z)


def over_core(x, c, y, z):
    return (x, 1 - c, y, z)


def over_z(step):
    return lambda x, c, y, z: (x, c, y, z ^ step)


def nt(a, b):
    return lax.dot_general(a, b, (((1,), (1,)), ((), ())), preferred_element_type=F32)


def nn(a, b):
    return lax.dot_general(a, b, (((1,), (0,)), ((), ())), preferred_element_type=F32)


def tn(a, b):
    return lax.dot_general(a, b, (((0,), (0,)), ((), ())), preferred_element_type=F32)


def near_call(kernel, info, args, outs, limit, in_hbm=False, out_hbm=False, scratch=()):
    vmem = pl.BlockSpec(memory_space=pltpu.VMEM)
    wide = pl.BlockSpec(memory_space=pltpu.HBM)
    space = pltpu.HBM if in_hbm else pltpu.VMEM
    args = [pltpu.with_memory_space_constraint(a, space) for a in args]
    shapes = [
        jax.ShapeDtypeStruct(s, d) if out_hbm else pltpu.VMEM(s, d) for s, d in outs
    ]
    return pl.pallas_call(
        kernel,
        in_specs=[pl.BlockSpec(memory_space=pltpu.SMEM)]
        + [wide if in_hbm else vmem] * len(args),
        out_specs=[vmem] * len(outs),
        out_shape=shapes,
        scratch_shapes=list(scratch),
        compiler_params=pltpu.CompilerParams(vmem_limit_bytes=limit * 1024 * 1024),
    )(info, *args)


def lanes(start, size):
    return pl.ds(pl.multiple_of(start, HEAD_DIM), size)


def rows_of(block, size):
    return pl.ds(pl.multiple_of(block * size, size), size)


def split_weights_kernel(
    info, weight, cross_rest, cross_both, own_rest, own_both, own_other, sem
):
    x, y = info[0], info[2]
    half = weight.shape[1] // 2
    shared = SHARED_COLS
    rest = half - shared
    there, here = (1 - y) * half, y * half
    copies = []
    for row, first, width, to in (
        (x * 128, there + shared, rest, cross_rest),
        (0, there, shared, cross_both.at[:, :shared]),
        (128, there, shared, cross_both.at[:, shared:]),
        (x * 128, here + shared, rest, own_rest),
        (0, here, shared, own_both.at[:, :shared]),
        (128, here, shared, own_both.at[:, shared:]),
        ((1 - x) * 128, here + shared, rest, own_other),
    ):
        source = weight.at[lanes(row, 128), lanes(first, width)]
        copies.append(pltpu.make_async_copy(source, to, sem.at[len(copies)]))
    for copy in copies:
        copy.start()
    for copy in copies:
        copy.wait()


def split_grad_kernel(info, grad, give, keep, sem):
    y = info[2]
    half = grad.shape[1] // 2
    copies = [
        pltpu.make_async_copy(grad.at[:, lanes((1 - y) * half, half)], give, sem.at[0]),
        pltpu.make_async_copy(grad.at[:, lanes(y * half, half)], keep, sem.at[1]),
    ]
    for copy in copies:
        copy.start()
    for copy in copies:
        copy.wait()


def split_heads_kernel(
    info, q, o, k, v, qo_give, qo_keep, k_give, k_keep, v_give, v_keep, sem
):
    c = info[1]
    copies = []
    for qo, keys, values, parity in (
        (qo_give, k_give, v_give, 1 - c),
        (qo_keep, k_keep, v_keep, c),
    ):
        for slot in range(4):
            head = 2 * slot + parity
            for source, to, start, width in (
                (k, keys, 0, 128),
                (v, values, 0, 128),
                (q, qo, 0, 256),
                (o, qo, 1024, 256),
            ):
                at = start + slot * width
                copies.append(
                    pltpu.make_async_copy(
                        source.at[:, lanes(head * width, width)],
                        to.at[:, at : at + width],
                        sem.at[len(copies)],
                    )
                )
    for copy in copies:
        copy.start()
    for copy in copies:
        copy.wait()


def pick_kernel(info, own, got, out):
    out[...] = jnp.where(info[1] == info[2], own[...], got[...])


def head_part_kernel(info, give_own, give_other, keep_own, keep_other, both, *refs, which):
    x, c = info[0], info[1]
    rows = give_own.shape[0]
    shared = SHARED_COLS
    weights = refs[: len(which)]
    give, keep = refs[len(which) :]
    first = both[:, :shared]
    second = both[:, shared:]
    common = [
        jnp.where(x == 0, first, second) if i == 0 else jnp.where(x == 0, second, first)
        for i in which
    ]
    rest = [w[...] for w in weights]
    if len(which) == 2:
        common = [jnp.concatenate(common, axis=0)]
        rest = [jnp.concatenate(rest, axis=0)]
    for grad, block, out in (
        (give_own, c, give),
        (give_other, 1 - c, give),
        (keep_own, c, keep),
        (keep_other, 1 - c, keep),
    ):
        total = nt(grad[:, shared:], rest[0]) + nt(grad[:, :shared], common[0])
        out[pl.ds(pl.multiple_of(block * rows, rows), rows), :] = total.astype(out.dtype)


def in_order(c, mine, other):
    first = jnp.where(c == 0, mine, other)
    second = jnp.where(c == 0, other, mine)
    return first, second


def col_max(a):
    return jnp.max(a, axis=0, keepdims=True)


def col_sum(a):
    return jnp.sum(a, axis=0, keepdims=True)


def probs_kernel(info, qo, qo_got, k, k_got, far, far_got, pd, px, *, steps):
    x, c = info[0], info[1]
    b = qo.shape[0]
    scale = score_scale
    key = lax.broadcasted_iota(jnp.int32, (b, b), 0)
    token = lax.broadcasted_iota(jnp.int32, (b, b), 1)
    seen = key <= token

    for n, step in enumerate(steps):
        slot = info[3] ^ step
        key_at = lanes(slot * HEAD_DIM, HEAD_DIM)
        key0, key1 = in_order(c, k[:, key_at], k_got[:, key_at])
        for head in range(2):
            at = lanes(slot * 256 + head * HEAD_DIM, HEAD_DIM)
            q0, q1 = in_order(c, qo[:, at], qo_got[:, at])
            s00 = jnp.where(seen, nt(key0, q0) * scale, masked_value)
            s01 = nt(key0, q1) * scale
            s11 = jnp.where(seen, nt(key1, q1) * scale, masked_value)
            m0 = col_max(s00)
            m1 = jnp.maximum(col_max(s01), col_max(s11))

            def store(m0, m1, more0, more1, inverse):
                e00 = jnp.exp(s00 - m0)
                e01 = jnp.exp(s01 - m1)
                e11 = jnp.exp(s11 - m1)
                i0 = 1.0 / (col_sum(e00) + more0)
                i1 = 1.0 / (col_sum(e01) + col_sum(e11) + more1)
                pd[n, head, 0:b, 0:b] = (e00 * i0).astype(BF)
                pd[n, head, 0:b, b:] = (e01 * i1).astype(BF)
                pd[n, head, b:, b:] = (e11 * i1).astype(BF)
                inverse(i0, i1)

            @pl.when(x == 0)
            def _():
                store(m0, m1, 0.0, 0.0, lambda i0, i1: None)

            @pl.when(x == 1)
            def _():
                f0, f1 = in_order(c, far[:, key_at], far_got[:, key_at])
                t0 = [nt(f, q0) * scale for f in (f0, f1)]
                t1 = [nt(f, q1) * scale for f in (f0, f1)]
                n0 = jnp.maximum(m0, jnp.maximum(col_max(t0[0]), col_max(t0[1])))
                n1 = jnp.maximum(m1, jnp.maximum(col_max(t1[0]), col_max(t1[1])))
                g0 = [jnp.exp(t - n0) for t in t0]
                g1 = [jnp.exp(t - n1) for t in t1]

                def far_store(i0, i1):
                    for i in range(2):
                        px[n, head, i * b : (i + 1) * b, 0:b] = (g0[i] * i0).astype(BF)
                        px[n, head, i * b : (i + 1) * b, b:] = (g1[i] * i1).astype(BF)

                store(
                    n0,
                    n1,
                    col_sum(g0[0]) + col_sum(g0[1]),
                    col_sum(g1[0]) + col_sum(g1[1]),
                    far_store,
                )


def grads_kernel(
    info, own, back, qo, qo_got, k, k_got, v, v_got, far_k, far_k_got, far_v, far_v_got, pd, px,
    *refs, step, which
):
    x, c = info[0], info[1]
    slot = info[3] ^ step
    last = 1 in which
    carried = last and 0 not in which
    if carried:
        near_in, far_in, *refs = refs
    if last:
        dq, near, *far_low, far = refs
    else:
        dq, near, far = refs
    b = qo.shape[0]
    scale = score_scale
    key_at = lanes(slot * HEAD_DIM, HEAD_DIM)
    key0, key1 = in_order(c, k[:, key_at], k_got[:, key_at])
    value0, value1 = in_order(c, v[:, key_at], v_got[:, key_at])

    def put(to, at, dkey, dvalue, i):
        if i == 1:
            source = near_in if carried and to is near else far_in if carried else to
            dkey = (source[at, :HEAD_DIM] + dkey) * scale
            dvalue = source[at, HEAD_DIM:] + dvalue
        to[at, :HEAD_DIM] = dkey
        to[at, HEAD_DIM:] = dvalue

    for place_in, i in enumerate(which):
        head = i ^ x
        here = slice(place_in * HEAD_DIM, (place_in + 1) * HEAD_DIM)
        q_at = lanes(slot * 256 + head * HEAD_DIM, HEAD_DIM)
        out_at = lanes(1024 + slot * 256 + head * HEAD_DIM, HEAD_DIM)
        head_grad = (own[:, here] + back[:, here].astype(F32)).astype(BF)
        query = jnp.concatenate(in_order(c, qo[:, q_at], qo_got[:, q_at]), axis=0)
        out = jnp.concatenate(in_order(c, qo[:, out_at], qo_got[:, out_at]), axis=0)
        product = head_grad.astype(F32) * out.astype(F32)
        delta = col_sum(jnp.transpose(product)).astype(BF).astype(F32)
        p0 = pd[step % 2, head, 0:b, :]
        p1 = pd[step % 2, head, b:, b:]
        d0 = (p0.astype(F32) * (nt(value0, head_grad) - delta)).astype(BF)
        d1 = (p1.astype(F32) * (nt(value1, head_grad[b:]) - delta[:, b:])).astype(BF)
        put(near, slice(0, b), nn(d0, query), nn(p0, head_grad), i)
        put(near, slice(b, 2 * b), nn(d1, query[b:]), nn(p1, head_grad[b:]), i)
        dq0 = tn(d0, key0)
        dq1 = dq0[b:] + tn(d1, key1)
        to = lanes(head * HEAD_DIM, HEAD_DIM) if len(which) == 2 else slice(0, HEAD_DIM)

        @pl.when(x == 0)
        def _():
            dq[0:b, to] = (dq0[:b] * scale).astype(BF)
            dq[b:, to] = (dq1 * scale).astype(BF)

        @pl.when(x == 1)
        def _():
            far_key = jnp.concatenate(in_order(c, far_k[:, key_at], far_k_got[:, key_at]), axis=0)
            far_value = jnp.concatenate(
                in_order(c, far_v[:, key_at], far_v_got[:, key_at]), axis=0
            )
            pf = px[step % 2, head]
            df = (pf.astype(F32) * (nt(far_value, head_grad) - delta)).astype(BF)
            dqf = tn(df, far_key)
            dq[0:b, to] = ((dq0[:b] + dqf[:b]) * scale).astype(BF)
            dq[b:, to] = ((dq1 + dqf[b:]) * scale).astype(BF)
            put(far, slice(0, 2 * b), nn(df, query), nn(pf, head_grad), i)

    if last:

        @pl.when(x == 1)
        def _():
            if len(far_low) == 1:
                far_low[0][...] = far[...].astype(BF)
            else:
                for block, out in ((c, far_low[0]), (1 - c, far_low[1])):
                    out[...] = far[rows_of(block, b), :].astype(BF)


def merge_kernel(info, dq, near, from_far, mine, crossed):
    x, c = info[0], info[1]
    b = mine.shape[0]
    for at, out in ((rows_of(c, b), mine), (rows_of(1 - c, b), crossed)):
        out[:, :256] = dq[at, :]
        more = jnp.where(x == 0, from_far[at, :].astype(F32), 0.0)
        out[:, 256:] = (near[at, :] + more).astype(BF)


def cross_kernel(info, dq_first, dq_second, near, crossed):
    x, c = info[0], info[1]
    b = crossed.shape[0]
    at = rows_of(1 - c, b)
    for i, dq in enumerate((dq_first, dq_second)):
        crossed[:, lanes((i ^ x) * HEAD_DIM, HEAD_DIM)] = dq[at, :]
    crossed[:, 256:] = near[at, :].astype(BF)


def finish_kernel(info, *refs):
    query_out, key_out, value_out = refs[-3:]
    parts = refs[:-3]
    c, z = info[1], info[3]
    for r in range(len(parts) // 2):
        slot = z ^ r
        for part, parity in ((parts[2 * r], c), (parts[2 * r + 1], 1 - c)):
            head = 2 * slot + parity
            query_out[:, lanes(head * 256, 256)] = part[:, :256]
            key_out[:, lanes(head * HEAD_DIM, HEAD_DIM)] = part[:, 256 : 256 + HEAD_DIM]
            value_out[:, lanes(head * HEAD_DIM, HEAD_DIM)] = part[:, 256 + HEAD_DIM :]


def last_kernel(
    info, dq_first, dq_second, near, crossed, far_mine, far_theirs, q_in, k_in, v_in,
    query_out, key_out, value_out, mine, theirs, sem,
):
    x, c = info[0], info[1]
    slot = info[3] ^ 3
    b = mine.shape[0]
    at = rows_of(c, b)
    for i, dq in enumerate((dq_first, dq_second)):
        mine[:, lanes((i ^ x) * HEAD_DIM, HEAD_DIM)] = dq[at, :]
    theirs[:, :256] = crossed[:, :256]
    copies = []

    def out(part, parity, source, to, width):
        head = 2 * slot + parity
        copy = pltpu.make_async_copy(
            part.at[:, source : source + width], to.at[:, lanes(head * width, width)],
            sem.at[len(copies)],
        )
        copy.start()
        copies.append(copy)

    out(mine, c, 0, query_out, 256)
    out(theirs, 1 - c, 0, query_out, 256)
    more = jnp.where(x == 0, far_mine[...].astype(F32), 0.0)
    mine[:, 256:] = (near[at, :] + more).astype(BF)
    more = jnp.where(x == 0, far_theirs[...].astype(F32), 0.0)
    theirs[:, 256:] = (crossed[:, 256:].astype(F32) + more).astype(BF)
    for part, parity in ((mine, c), (theirs, 1 - c)):
        out(part, parity, 256, key_out, HEAD_DIM)
        out(part, parity, 256 + HEAD_DIM, value_out, HEAD_DIM)
    for copy in copies:
        copy.wait()


def fast_body(queries, projected_keys, projected_values, attention_result, output_grad, out_weight):
    q, k, v, o, og = (
        a[0]
        for a in (queries, projected_keys, projected_values, attention_result, output_grad)
    )
    rows = q.shape[0]
    half = og.shape[1] // 2
    shared = SHARED_COLS
    rest = half - shared
    dp = lax.axis_index("dp")
    ctx = lax.axis_index("ctx")
    z, y = dp // 2, dp % 2
    x, c = ctx // 2, ctx % 2
    info = jnp.stack([x, c, y, z]).astype(jnp.int32)
    dma = pltpu.SemaphoreType.DMA

    thin = ((128, rest), BF)
    both = ((128, 2 * shared), BF)
    cross_rest, cross_both, own_rest, own_both, own_other = near_call(
        split_weights_kernel, info, [out_weight], [thin, both, thin, both, thin],
        8, in_hbm=True, scratch=[dma((7,))],
    )
    to_other = lambda x, c, y, z: (x, c, 1 - y, z) if y == c else None
    got_rest = send(cross_rest, to_other)
    got_both = send(cross_both, to_other)

    def pick(own, got, shape):
        return near_call(pick_kernel, info, [own, got], [shape], 8)[0]

    half_grad = ((rows, half), BF)
    og_give, og_keep = near_call(
        split_grad_kernel, info, [og], [half_grad, half_grad], 8,
        in_hbm=PREFETCH, scratch=[dma((2,))],
    )
    qo_give, qo_keep, k_give, k_keep, v_give, v_keep = near_call(
        split_heads_kernel, info, [q, o, k, v],
        [((rows, 2048), BF)] * 2 + [((rows, 512), BF)] * 4, 8,
        in_hbm=PREFETCH, scratch=[dma((32,))],
    )
    over_x_and_core = lambda x, c, y, z: (1 - x, 1 - c, y, z)
    far_k = send(k_keep, over_x)
    far_k_got = send(k_give, over_x_and_core)
    far_v = send(v_keep, over_x)
    far_v_got = send(v_give, over_x_and_core)
    k_got = send(k_give, over_core)
    v_got = send(v_give, over_core)
    qo_got = send(qo_give, over_core)
    keep_core = send(og_keep, over_core)
    give_back = send(og_give, over_y)
    give_core = send(give_back, over_core)

    w_rest = pick(own_rest, got_rest, thin)
    w_both = pick(own_both, got_both, both)
    rests, boths = [w_rest], [w_both]
    for step in (1, 2):
        if EARLY_Z:
            first = lambda x, c, y, z, step=step: (x, c, y, z ^ step) if y == c else None
            later = lambda x, c, y, z, step=step: (x, c, y, z ^ step) if y != c else None
            early = send(own_rest, first)
            late = send(got_rest, later)
            rests.append(pick(early, late, thin))
        else:
            rests.append(send(w_rest, over_z(step)))
        boths.append(send(w_both, over_z(step)))
    rests.append(send(rests[2], over_z(1)))
    boths.append(send(boths[2], over_z(1)))

    pair = ((2, 2, 2 * rows, 2 * rows), BF)
    probs = [
        near_call(
            functools.partial(probs_kernel, steps=steps), info,
            [qo_keep, qo_got, k_keep, k_got, far_k, far_k_got], [pair, pair], 16,
        )
        for steps in ((0, 1), (2, 3))
    ]

    def part(r, which, weights):
        width = HEAD_DIM * len(which)
        return near_call(
            functools.partial(head_part_kernel, which=which), info,
            [give_back, give_core, og_keep, keep_core, boths[r]] + weights,
            [((2 * rows, width), BF), ((2 * rows, width), F32)], 16,
        )

    def grads(r, which, keep, back, carry):
        key_sums = ((2 * rows, 256), F32)
        far_shapes = {1: [((rows, 256), BF)] * 2, 2: [((2 * rows, 256), BF)]}
        last = 1 in which
        return near_call(
            functools.partial(grads_kernel, step=r, which=which), info,
            [keep, back, qo_keep, qo_got, k_keep, k_got, v_keep, v_got]
            + [far_k, far_k_got, far_v, far_v_got] + list(probs[r // 2]) + carry,
            [((2 * rows, HEAD_DIM * len(which)), BF), key_sums]
            + (far_shapes[len(which)] if last else [key_sums]), 16,
            scratch=[pltpu.VMEM(*key_sums)] if last else [],
        )

    finals = []
    for r in range(4):
        if r == 0:
            crossed_only = lambda x, c, y, z: (1 - x, c, y, z) if y != c else None
            other = pick(own_other, send(w_rest, crossed_only), thin)
        else:
            other = send(rests[r], over_x)
        split = r == 3
        groups = ((0,), (1,)) if split else ((0, 1),)
        carry = []
        dqs = []
        for which in groups:
            weights = [(rests[r], other)[i] for i in which]
            give, keep = part(r, which, weights)
            back = send(give, over_y)
            dq, near, *far = grads(r, which, keep, back, carry)
            carry = [near] + far
            dqs.append(dq)
        if not split:
            from_far = send(far[0], over_x)
            ours, crossed = near_call(
                merge_kernel, info, dqs + [near, from_far], [((rows, 512), BF)] * 2, 8
            )
            finals += [ours, send(crossed, over_core)]

    far_mine = send(far[0], over_x)
    far_theirs = send(far[1], over_x_and_core)
    (crossed,) = near_call(cross_kernel, info, dqs + [near], [((rows, 512), BF)], 8)
    crossed = send(crossed, over_core)
    partial = near_call(
        finish_kernel, info, finals, [(a.shape, BF) for a in (q, k, v)], 16, out_hbm=True
    )
    vmem = pl.BlockSpec(memory_space=pltpu.VMEM)
    hbm = pl.BlockSpec(memory_space=pltpu.HBM)
    held = [
        pltpu.with_memory_space_constraint(a, pltpu.VMEM)
        for a in dqs + [near, crossed, far_mine, far_theirs]
    ]
    outs = pl.pallas_call(
        last_kernel,
        in_specs=[pl.BlockSpec(memory_space=pltpu.SMEM)] + [vmem] * 6 + [hbm] * 3,
        out_specs=[hbm] * 3,
        out_shape=[jax.ShapeDtypeStruct(a.shape, BF) for a in (q, k, v)],
        scratch_shapes=[pltpu.VMEM((rows, 512), BF)] * 2 + [dma((6,))],
        input_output_aliases={7: 0, 8: 1, 9: 2},
        compiler_params=pltpu.CompilerParams(vmem_limit_bytes=8 * 1024 * 1024),
        name="last",
    )(info, *held, *partial)
    return tuple(a[None] for a in outs)


def fits_fast(mesh):
    return dict(mesh.shape) == {"dp": 8, "ctx": 4}


def chosen_body(mesh):
    def run(queries, projected_keys, projected_values, attention_result, output_grad, out_weight):
        fast = (
            fits_fast(mesh)
            and queries.shape == (1, 256, 2048)
            and out_weight.shape[0] == 256
            and projected_keys.shape == (1, 256, 1024)
            and output_grad.shape[2] % 256 == 0
            and output_grad.shape[2] // 2 > SHARED_COLS
        )
        use = fast_body if fast else body
        return use(
            queries, projected_keys, projected_values, attention_result, output_grad, out_weight
        )

    return run


def solution(mesh):
    placed = (
        P("dp", "ctx", None),
        P("dp", "ctx", None),
        P("dp", "ctx", None),
        P("dp", "ctx", None),
        P("dp", "ctx", None),
        P("dp", None),
    )
    step = jax.shard_map(
        chosen_body(mesh),
        mesh=mesh,
        in_specs=placed,
        out_specs=(P("dp", "ctx", None), P("dp", "ctx", None), P("dp", "ctx", None)),
        check_vma=False,
    )
    if not fits_fast(mesh):
        return step
    return step
```

```python
import functools

import jax
import jax.numpy as jnp
from jax import lax
from jax.experimental import pallas as pl
from jax.experimental.pallas import tpu as pltpu
from jax.sharding import PartitionSpec as P


KEY_HEAD_COUNT = 8
HEAD_DIM = 128
WINDOW = 1024


score_scale = 168.0 ** (-0.5)
masked_value = -1e30


def band_backward(
    query_head_total, key_head_total, value_head_total, gradient_by_head, delta_heads
):
    sequence_tokens, local_kv, query_feature_width = query_head_total.shape
    head_size = key_head_total.shape[2]
    queries_per_group = query_feature_width // head_size
    block_rows = min(512, sequence_tokens)
    span_len = WINDOW + block_rows
    query_four = query_head_total.reshape(sequence_tokens, local_kv, queries_per_group, head_size)
    gradient_rank_four = gradient_by_head.reshape(
        sequence_tokens, local_kv, queries_per_group, head_size
    )
    leading = jnp.zeros((WINDOW, local_kv, head_size), key_head_total.dtype)
    key_padded = jnp.concatenate([leading, key_head_total], axis=0)
    value_padded = jnp.concatenate([leading, value_head_total], axis=0)
    delta_float = delta_heads.astype(jnp.float32)

    def one_block(block_index, totals):
        query_total, key_total, value_total = totals
        first_row = (block_index * block_rows).astype(jnp.int32)
        query_block = lax.dynamic_slice_in_dim(query_four, first_row, block_rows, 0)
        grad_block = lax.dynamic_slice_in_dim(gradient_rank_four, first_row, block_rows, 0)
        delta_block = lax.dynamic_slice_in_dim(delta_float, first_row, block_rows, 0)
        key_block = lax.dynamic_slice_in_dim(key_padded, first_row, span_len, 0)
        value_block = lax.dynamic_slice_in_dim(value_padded, first_row, span_len, 0)
        scores = (
            jnp.einsum("qhgd,khd->hgqk", query_block, key_block, preferred_element_type=jnp.float32)
            * score_scale
        )
        query_pos = first_row + lax.iota(jnp.int32, block_rows)
        key_pos = first_row - WINDOW + lax.iota(jnp.int32, span_len)
        visible = (
            (key_pos[None, :] <= query_pos[:, None])
            & (key_pos[None, :] > query_pos[:, None] - WINDOW)
            & (key_pos[None, :] >= 0)
        )
        scores = jnp.where(visible, scores, masked_value)
        highest = jnp.max(scores, axis=-1, keepdims=True)
        expos = jnp.exp(scores - highest)
        probs = expos / jnp.sum(expos, axis=-1, keepdims=True)
        probs_low = probs.astype(jnp.bfloat16)
        dprobs = jnp.einsum(
            "qhgd,khd->hgqk", grad_block, value_block, preferred_element_type=jnp.float32
        )
        delta_rows = jnp.transpose(delta_block, (1, 2, 0))[..., None]
        dscores = (probs * (dprobs - delta_rows)).astype(jnp.bfloat16)
        query_part = (
            jnp.einsum("hgqk,khd->qhgd", dscores, key_block, preferred_element_type=jnp.float32)
            * score_scale
        )
        key_portion = (
            jnp.einsum("hgqk,qhgd->khd", dscores, query_block, preferred_element_type=jnp.float32)
            * score_scale
        )
        value_portion = jnp.einsum(
            "hgqk,qhgd->khd", probs_low, grad_block, preferred_element_type=jnp.float32
        )
        query_total = lax.dynamic_update_slice_in_dim(
            query_total, query_part.reshape(block_rows, local_kv, query_feature_width), first_row, 0
        )
        key_total = lax.dynamic_update_slice_in_dim(
            key_total,
            lax.dynamic_slice_in_dim(key_total, first_row, span_len, 0) + key_portion,
            first_row,
            0,
        )
        value_total = lax.dynamic_update_slice_in_dim(
            value_total,
            lax.dynamic_slice_in_dim(value_total, first_row, span_len, 0) + value_portion,
            first_row,
            0,
        )
        return (query_total, key_total, value_total)

    initial = (
        jnp.zeros((sequence_tokens, local_kv, query_feature_width), jnp.float32),
        jnp.zeros((WINDOW + sequence_tokens, local_kv, head_size), jnp.float32),
        jnp.zeros((WINDOW + sequence_tokens, local_kv, head_size), jnp.float32),
    )
    query_total, key_total, value_total = lax.fori_loop(
        0, sequence_tokens // block_rows, one_block, initial
    )
    return (
        query_total.astype(jnp.bfloat16),
        key_total[WINDOW:].astype(jnp.bfloat16),
        value_total[WINDOW:].astype(jnp.bfloat16),
    )


def head_delta(gradient_rank_three, output_rank_three):
    rows_here, heads_here, query_feature_width = gradient_rank_three.shape
    queries_per_group = query_feature_width // HEAD_DIM
    gradient_rank_four = gradient_rank_three.reshape(
        rows_here, heads_here, queries_per_group, HEAD_DIM
    ).astype(jnp.float32)
    output_rank_four = output_rank_three.reshape(
        rows_here, heads_here, queries_per_group, HEAD_DIM
    ).astype(jnp.float32)
    return jnp.sum(gradient_rank_four * output_rank_four, axis=-1).astype(jnp.bfloat16)


def one_sequence(query_rows, key_rows, value_rows, output_rows, gradient_rows):
    token_total = query_rows.shape[0]
    query_feature_width = query_rows.shape[1]
    queries_per_group = query_feature_width // (KEY_HEAD_COUNT * HEAD_DIM)
    query_rank_three = query_rows.reshape(token_total, KEY_HEAD_COUNT, queries_per_group * HEAD_DIM)
    key_rank_three = key_rows.reshape(token_total, KEY_HEAD_COUNT, HEAD_DIM)
    value_rank_three = value_rows.reshape(token_total, KEY_HEAD_COUNT, HEAD_DIM)
    output_rank_three = output_rows.reshape(
        token_total, KEY_HEAD_COUNT, queries_per_group * HEAD_DIM
    )
    gradient_rank_three = gradient_rows.reshape(
        token_total, KEY_HEAD_COUNT, queries_per_group * HEAD_DIM
    )
    query_head_total, key_head_total, value_head_total, output_heads = (
        lax.all_to_all(query_rank_three, "ctx", split_axis=1, concat_axis=0, tiled=True),
        lax.all_to_all(key_rank_three, "ctx", split_axis=1, concat_axis=0, tiled=True),
        lax.all_to_all(value_rank_three, "ctx", split_axis=1, concat_axis=0, tiled=True),
        lax.all_to_all(output_rank_three, "ctx", split_axis=1, concat_axis=0, tiled=True),
    )
    gradient_by_head = lax.all_to_all(
        gradient_rank_three, "ctx", split_axis=1, concat_axis=0, tiled=True
    )
    delta_heads = head_delta(gradient_by_head, output_heads)
    query_back, key_back, value_back = band_backward(
        query_head_total, key_head_total, value_head_total, gradient_by_head, delta_heads
    )
    query_local, key_slice_here, value_slice_here = (
        lax.all_to_all(query_back, "ctx", split_axis=0, concat_axis=1, tiled=True),
        lax.all_to_all(key_back, "ctx", split_axis=0, concat_axis=1, tiled=True),
        lax.all_to_all(value_back, "ctx", split_axis=0, concat_axis=1, tiled=True),
    )
    return (
        query_local.reshape(token_total, query_feature_width),
        key_slice_here.reshape(token_total, KEY_HEAD_COUNT * HEAD_DIM),
        value_slice_here.reshape(token_total, KEY_HEAD_COUNT * HEAD_DIM),
    )


def body(queries, projected_keys, projected_values, attention_result, output_grad, out_weight):
    sequences_here = queries.shape[0]
    token_total = queries.shape[1]
    query_feature_width = queries.shape[2]
    row_total = sequences_here * token_total
    grad_rows = output_grad.reshape(row_total, output_grad.shape[2])
    per_head_gradient = lax.dot_general(
        grad_rows,
        lax.all_gather(out_weight, "dp", axis=0, tiled=True),
        (((1,), (1,)), ((), ())),
        preferred_element_type=jnp.float32,
    ).astype(jnp.bfloat16)
    per_head_gradient = per_head_gradient.reshape(sequences_here, token_total, query_feature_width)
    query_part, key_part, value_part = one_sequence(
        queries[0],
        projected_keys[0],
        projected_values[0],
        attention_result[0],
        per_head_gradient[0],
    )
    query_list = [query_part]
    key_list = [key_part]
    value_list = [value_part]
    return (
        jnp.stack(query_list, axis=0),
        jnp.stack(key_list, axis=0),
        jnp.stack(value_list, axis=0),
    )


AXES = ("dp", "ctx")
SHARED_COLS = 640
BF = jnp.bfloat16
F32 = jnp.float32


def place(x, c, y, z):
    return (z * 2 + y) * 4 + x * 2 + c


def pairs(target):
    found = []
    for z in range(4):
        for y in range(2):
            for x in range(2):
                for c in range(2):
                    to = target(x, c, y, z)
                    if to is not None:
                        found.append((place(x, c, y, z), place(*to)))
    return found


def send(value, target):
    return lax.ppermute(value, AXES, pairs(target))


def over_x(x, c, y, z):
    return (1 - x, c, y, z)


def over_y(x, c, y, z):
    return (x, c, 1 - y, z)


def over_core(x, c, y, z):
    return (x, 1 - c, y, z)


def over_z(step):
    return lambda x, c, y, z: (x, c, y, z ^ step)


def nt(a, b):
    return lax.dot_general(a, b, (((1,), (1,)), ((), ())), preferred_element_type=F32)


def nn(a, b):
    return lax.dot_general(a, b, (((1,), (0,)), ((), ())), preferred_element_type=F32)


def tn(a, b):
    return lax.dot_general(a, b, (((0,), (0,)), ((), ())), preferred_element_type=F32)


def near_call(kernel, info, args, outs, limit, in_hbm=False, out_hbm=False, scratch=()):
    vmem = pl.BlockSpec(memory_space=pltpu.VMEM)
    wide = pl.BlockSpec(memory_space=pltpu.HBM)
    space = pltpu.HBM if in_hbm else pltpu.VMEM
    args = [pltpu.with_memory_space_constraint(a, space) for a in args]
    shapes = [
        jax.ShapeDtypeStruct(s, d) if out_hbm else pltpu.VMEM(s, d) for s, d in outs
    ]
    return pl.pallas_call(
        kernel,
        in_specs=[pl.BlockSpec(memory_space=pltpu.SMEM)]
        + [wide if in_hbm else vmem] * len(args),
        out_specs=[vmem] * len(outs),
        out_shape=shapes,
        scratch_shapes=list(scratch),
        compiler_params=pltpu.CompilerParams(vmem_limit_bytes=limit * 1024 * 1024),
    )(info, *args)


def lanes(start, size):
    return pl.ds(pl.multiple_of(start, HEAD_DIM), size)


def rows_of(block, size):
    return pl.ds(pl.multiple_of(block * size, size), size)


def cut_weights_kernel(info, weight, *refs, own):
    *outs, sem = refs
    x, y = info[0], info[2]
    half = weight.shape[1] // 2
    shared = SHARED_COLS
    first = (y if own else 1 - y) * half
    jobs = [
        (x * 128, first + shared, half - shared, outs[0]),
        (0, first, shared, outs[1].at[:, :shared]),
        (128, first, shared, outs[1].at[:, shared:]),
    ]
    if own:
        jobs.append(((1 - x) * 128, first + shared, half - shared, outs[2]))
    copies = [
        pltpu.make_async_copy(weight.at[lanes(row, 128), lanes(at, width)], to, sem.at[i])
        for i, (row, at, width, to) in enumerate(jobs)
    ]
    for copy in copies:
        copy.start()
    for copy in copies:
        copy.wait()


def split_grad_kernel(info, grad, give, keep, sem):
    y = info[2]
    half = grad.shape[1] // 2
    copies = [
        pltpu.make_async_copy(grad.at[:, lanes((1 - y) * half, half)], give, sem.at[0]),
        pltpu.make_async_copy(grad.at[:, lanes(y * half, half)], keep, sem.at[1]),
    ]
    for copy in copies:
        copy.start()
    for copy in copies:
        copy.wait()


def split_heads_kernel(
    info, q, o, k, v, qo_give, qo_keep, k_give, k_keep, v_give, v_keep, sem
):
    c = info[1]
    copies = []
    for qo, keys, values, parity in (
        (qo_give, k_give, v_give, 1 - c),
        (qo_keep, k_keep, v_keep, c),
    ):
        for slot in range(4):
            head = 2 * slot + parity
            for source, to, start, width in (
                (k, keys, 0, 128),
                (v, values, 0, 128),
                (q, qo, 0, 256),
                (o, qo, 1024, 256),
            ):
                at = start + slot * width
                copies.append(
                    pltpu.make_async_copy(
                        source.at[:, lanes(head * width, width)],
                        to.at[:, at : at + width],
                        sem.at[len(copies)],
                    )
                )
    for copy in copies:
        copy.start()
    for copy in copies:
        copy.wait()


def pick_kernel(info, own, got, out):
    out[...] = jnp.where(info[1] == info[2], own[...], got[...])


def head_part_kernel(info, *refs, which, sides):
    x, c = info[0], info[1]
    shared = SHARED_COLS
    grads, refs = refs[: 2 * sides], refs[2 * sides :]
    both, *weights = refs[: 1 + len(which)]
    outs = refs[1 + len(which) :]
    rows = grads[0].shape[0]
    first = both[:, :shared]
    second = both[:, shared:]
    common = [
        jnp.where(x == 0, first, second) if i == 0 else jnp.where(x == 0, second, first)
        for i in which
    ]
    rest = [w[...] for w in weights]
    if len(which) == 2:
        common = [jnp.concatenate(common, axis=0)]
        rest = [jnp.concatenate(rest, axis=0)]
    for side, out in enumerate(outs):
        for grad, block in ((grads[2 * side], c), (grads[2 * side + 1], 1 - c)):
            total = nt(grad[:, shared:], rest[0]) + nt(grad[:, :shared], common[0])
            out[rows_of(block, rows), :] = total.astype(out.dtype)


def in_order(c, mine, other):
    first = jnp.where(c == 0, mine, other)
    second = jnp.where(c == 0, other, mine)
    return first, second


def col_max(a):
    return jnp.max(a, axis=0, keepdims=True)


def col_sum(a):
    return jnp.sum(a, axis=0, keepdims=True)


def probs_kernel(info, qo, qo_got, k, k_got, far, far_got, pd, px, *, steps):
    x, c = info[0], info[1]
    b = qo.shape[0]
    scale = score_scale
    key = lax.broadcasted_iota(jnp.int32, (b, b), 0)
    token = lax.broadcasted_iota(jnp.int32, (b, b), 1)
    seen = key <= token

    for n, step in enumerate(steps):
        slot = info[3] ^ step
        key_at = lanes(slot * HEAD_DIM, HEAD_DIM)
        key0, key1 = in_order(c, k[:, key_at], k_got[:, key_at])
        for head in range(2):
            at = lanes(slot * 256 + head * HEAD_DIM, HEAD_DIM)
            q0, q1 = in_order(c, qo[:, at], qo_got[:, at])
            s00 = jnp.where(seen, nt(key0, q0) * scale, masked_value)
            s01 = nt(key0, q1) * scale
            s11 = jnp.where(seen, nt(key1, q1) * scale, masked_value)
            m0 = col_max(s00)
            m1 = jnp.maximum(col_max(s01), col_max(s11))

            def store(m0, m1, more0, more1, inverse):
                e00 = jnp.exp(s00 - m0)
                e01 = jnp.exp(s01 - m1)
                e11 = jnp.exp(s11 - m1)
                i0 = 1.0 / (col_sum(e00) + more0)
                i1 = 1.0 / (col_sum(e01) + col_sum(e11) + more1)
                pd[n, head, 0:b, 0:b] = (e00 * i0).astype(BF)
                pd[n, head, 0:b, b:] = (e01 * i1).astype(BF)
                pd[n, head, b:, b:] = (e11 * i1).astype(BF)
                inverse(i0, i1)

            @pl.when(x == 0)
            def _():
                store(m0, m1, 0.0, 0.0, lambda i0, i1: None)

            @pl.when(x == 1)
            def _():
                f0, f1 = in_order(c, far[:, key_at], far_got[:, key_at])
                t0 = [nt(f, q0) * scale for f in (f0, f1)]
                t1 = [nt(f, q1) * scale for f in (f0, f1)]
                n0 = jnp.maximum(m0, jnp.maximum(col_max(t0[0]), col_max(t0[1])))
                n1 = jnp.maximum(m1, jnp.maximum(col_max(t1[0]), col_max(t1[1])))
                g0 = [jnp.exp(t - n0) for t in t0]
                g1 = [jnp.exp(t - n1) for t in t1]

                def far_store(i0, i1):
                    for i in range(2):
                        px[n, head, i * b : (i + 1) * b, 0:b] = (g0[i] * i0).astype(BF)
                        px[n, head, i * b : (i + 1) * b, b:] = (g1[i] * i1).astype(BF)

                store(
                    n0,
                    n1,
                    col_sum(g0[0]) + col_sum(g0[1]),
                    col_sum(g1[0]) + col_sum(g1[1]),
                    far_store,
                )


def grads_kernel(
    info, own, back, qo, qo_got, k, k_got, v, v_got, far_k, far_k_got, far_v, far_v_got, pd, px,
    *refs, step, which
):
    x, c = info[0], info[1]
    slot = info[3] ^ step
    last = 1 in which
    carried = last and 0 not in which
    if carried:
        near_in, far_in, *refs = refs
    if last:
        dq, near, *far_low, far = refs
    else:
        dq, near, far = refs
    b = qo.shape[0]
    scale = score_scale
    key_at = lanes(slot * HEAD_DIM, HEAD_DIM)
    key0, key1 = in_order(c, k[:, key_at], k_got[:, key_at])
    value0, value1 = in_order(c, v[:, key_at], v_got[:, key_at])

    def put(to, at, dkey, dvalue, i):
        if i == 1:
            source = near_in if carried and to is near else far_in if carried else to
            dkey = (source[at, :HEAD_DIM] + dkey) * scale
            dvalue = source[at, HEAD_DIM:] + dvalue
        to[at, :HEAD_DIM] = dkey
        to[at, HEAD_DIM:] = dvalue

    for place_in, i in enumerate(which):
        head = i ^ x
        here = slice(place_in * HEAD_DIM, (place_in + 1) * HEAD_DIM)
        q_at = lanes(slot * 256 + head * HEAD_DIM, HEAD_DIM)
        out_at = lanes(1024 + slot * 256 + head * HEAD_DIM, HEAD_DIM)
        head_grad = (own[:, here] + back[:, here].astype(F32)).astype(BF)
        query = jnp.concatenate(in_order(c, qo[:, q_at], qo_got[:, q_at]), axis=0)
        out = jnp.concatenate(in_order(c, qo[:, out_at], qo_got[:, out_at]), axis=0)
        product = head_grad.astype(F32) * out.astype(F32)
        delta = col_sum(jnp.transpose(product)).astype(BF).astype(F32)
        p0 = pd[step % 2, head, 0:b, :]
        p1 = pd[step % 2, head, b:, b:]
        d0 = (p0.astype(F32) * (nt(value0, head_grad) - delta)).astype(BF)
        d1 = (p1.astype(F32) * (nt(value1, head_grad[b:]) - delta[:, b:])).astype(BF)
        put(near, slice(0, b), nn(d0, query), nn(p0, head_grad), i)
        put(near, slice(b, 2 * b), nn(d1, query[b:]), nn(p1, head_grad[b:]), i)
        dq0 = tn(d0, key0)
        dq1 = dq0[b:] + tn(d1, key1)
        to = lanes(head * HEAD_DIM, HEAD_DIM) if len(which) == 2 else slice(0, HEAD_DIM)

        @pl.when(x == 0)
        def _():
            dq[0:b, to] = (dq0[:b] * scale).astype(BF)
            dq[b:, to] = (dq1 * scale).astype(BF)

        @pl.when(x == 1)
        def _():
            far_key = jnp.concatenate(in_order(c, far_k[:, key_at], far_k_got[:, key_at]), axis=0)
            far_value = jnp.concatenate(
                in_order(c, far_v[:, key_at], far_v_got[:, key_at]), axis=0
            )
            pf = px[step % 2, head]
            df = (pf.astype(F32) * (nt(far_value, head_grad) - delta)).astype(BF)
            dqf = tn(df, far_key)
            dq[0:b, to] = ((dq0[:b] + dqf[:b]) * scale).astype(BF)
            dq[b:, to] = ((dq1 + dqf[b:]) * scale).astype(BF)
            put(far, slice(0, 2 * b), nn(df, query), nn(pf, head_grad), i)

    if last:

        @pl.when(x == 1)
        def _():
            if len(far_low) == 1:
                far_low[0][...] = far[...].astype(BF)
            else:
                for block, out in ((c, far_low[0]), (1 - c, far_low[1])):
                    out[...] = far[rows_of(block, b), :].astype(BF)


def merge_kernel(info, dq, near, from_far, mine, crossed):
    x, c = info[0], info[1]
    b = mine.shape[0]
    for at, out in ((rows_of(c, b), mine), (rows_of(1 - c, b), crossed)):
        out[:, :256] = dq[at, :]
        more = jnp.where(x == 0, from_far[at, :].astype(F32), 0.0)
        out[:, 256:] = (near[at, :] + more).astype(BF)


def cross_kernel(info, dq_first, dq_second, near, crossed):
    x, c = info[0], info[1]
    b = crossed.shape[0]
    at = rows_of(1 - c, b)
    for i, dq in enumerate((dq_first, dq_second)):
        crossed[:, lanes((i ^ x) * HEAD_DIM, HEAD_DIM)] = dq[at, :]
    crossed[:, 256:] = near[at, :].astype(BF)


def finish_kernel(info, *refs):
    query_out, key_out, value_out = refs[-3:]
    parts = refs[:-3]
    c, z = info[1], info[3]
    for r in range(len(parts) // 2):
        slot = z ^ r
        for part, parity in ((parts[2 * r], c), (parts[2 * r + 1], 1 - c)):
            head = 2 * slot + parity
            query_out[:, lanes(head * 256, 256)] = part[:, :256]
            key_out[:, lanes(head * HEAD_DIM, HEAD_DIM)] = part[:, 256 : 256 + HEAD_DIM]
            value_out[:, lanes(head * HEAD_DIM, HEAD_DIM)] = part[:, 256 + HEAD_DIM :]


def last_kernel(
    info, dq_first, dq_second, near, crossed, far_mine, far_theirs, q_in, k_in, v_in,
    query_out, key_out, value_out, mine, theirs, sem,
):
    x, c = info[0], info[1]
    slot = info[3] ^ 3
    b = mine.shape[0]
    at = rows_of(c, b)
    for i, dq in enumerate((dq_first, dq_second)):
        mine[:, lanes((i ^ x) * HEAD_DIM, HEAD_DIM)] = dq[at, :]
    theirs[:, :256] = crossed[:, :256]
    copies = []

    def out(part, parity, source, to, width):
        head = 2 * slot + parity
        copy = pltpu.make_async_copy(
            part.at[:, source : source + width], to.at[:, lanes(head * width, width)],
            sem.at[len(copies)],
        )
        copy.start()
        copies.append(copy)

    out(mine, c, 0, query_out, 256)
    out(theirs, 1 - c, 0, query_out, 256)
    more = jnp.where(x == 0, far_mine[...].astype(F32), 0.0)
    mine[:, 256:] = (near[at, :] + more).astype(BF)
    more = jnp.where(x == 0, far_theirs[...].astype(F32), 0.0)
    theirs[:, 256:] = (crossed[:, 256:].astype(F32) + more).astype(BF)
    for part, parity in ((mine, c), (theirs, 1 - c)):
        out(part, parity, 256, key_out, HEAD_DIM)
        out(part, parity, 256 + HEAD_DIM, value_out, HEAD_DIM)
    for copy in copies:
        copy.wait()


def fast_body(queries, projected_keys, projected_values, attention_result, output_grad, out_weight):
    q, k, v, o, og = (
        a[0]
        for a in (queries, projected_keys, projected_values, attention_result, output_grad)
    )
    rows = q.shape[0]
    half = og.shape[1] // 2
    shared = SHARED_COLS
    rest = half - shared
    dp = lax.axis_index("dp")
    ctx = lax.axis_index("ctx")
    z, y = dp // 2, dp % 2
    x, c = ctx // 2, ctx % 2
    info = jnp.stack([x, c, y, z]).astype(jnp.int32)
    dma = pltpu.SemaphoreType.DMA

    thin = ((128, rest), BF)
    both = ((128, 2 * shared), BF)
    cross_rest, cross_both = near_call(
        functools.partial(cut_weights_kernel, own=False), info, [out_weight],
        [thin, both], 8, in_hbm=True, scratch=[dma((3,))],
    )
    own_rest, own_both, own_other = near_call(
        functools.partial(cut_weights_kernel, own=True), info, [out_weight],
        [thin, both, thin], 8, in_hbm=True, scratch=[dma((4,))],
    )
    to_other = lambda x, c, y, z: (x, c, 1 - y, z) if y == c else None
    got_rest = send(cross_rest, to_other)
    got_both = send(cross_both, to_other)

    def pick(own, got, shape):
        return near_call(pick_kernel, info, [own, got], [shape], 8)[0]

    half_grad = ((rows, half), BF)
    og_give, og_keep = near_call(
        split_grad_kernel, info, [og], [half_grad, half_grad], 8,
        scratch=[dma((2,))],
    )
    qo_give, qo_keep, k_give, k_keep, v_give, v_keep = near_call(
        split_heads_kernel, info, [q, o, k, v],
        [((rows, 2048), BF)] * 2 + [((rows, 512), BF)] * 4, 8,
        scratch=[dma((32,))],
    )
    over_x_and_core = lambda x, c, y, z: (1 - x, 1 - c, y, z)
    far_k = send(k_keep, over_x)
    far_k_got = send(k_give, over_x_and_core)
    far_v = send(v_keep, over_x)
    far_v_got = send(v_give, over_x_and_core)
    k_got = send(k_give, over_core)
    v_got = send(v_give, over_core)
    qo_got = send(qo_give, over_core)
    keep_core = send(og_keep, over_core)
    give_back = send(og_give, over_y)
    give_core = send(give_back, over_core)

    w_rest = pick(own_rest, got_rest, thin)
    w_both = pick(own_both, got_both, both)
    rests, boths = [w_rest], [w_both]
    for step in (1, 2):
        rests.append(send(w_rest, over_z(step)))
        boths.append(send(w_both, over_z(step)))
    rests.append(send(rests[2], over_z(1)))
    boths.append(send(boths[2], over_z(1)))

    pair = ((2, 2, 2 * rows, 2 * rows), BF)
    probs = [
        near_call(
            functools.partial(probs_kernel, steps=steps), info,
            [qo_keep, qo_got, k_keep, k_got, far_k, far_k_got], [pair, pair], 16,
        )
        for steps in ((0, 1), (2, 3))
    ]

    sides = {"give": ([give_back, give_core], BF), "keep": ([og_keep, keep_core], F32)}

    def part(r, which, weights, names):
        width = HEAD_DIM * len(which)
        return near_call(
            functools.partial(head_part_kernel, which=which, sides=len(names)), info,
            [a for n in names for a in sides[n][0]] + [boths[r]] + weights,
            [((2 * rows, width), sides[n][1]) for n in names], 16,
        )

    def grads(r, which, keep, back, carry):
        key_sums = ((2 * rows, 256), F32)
        far_shapes = {1: [((rows, 256), BF)] * 2, 2: [((2 * rows, 256), BF)]}
        last = 1 in which
        return near_call(
            functools.partial(grads_kernel, step=r, which=which), info,
            [keep, back, qo_keep, qo_got, k_keep, k_got, v_keep, v_got]
            + [far_k, far_k_got, far_v, far_v_got] + list(probs[r // 2]) + carry,
            [((2 * rows, HEAD_DIM * len(which)), BF), key_sums]
            + (far_shapes[len(which)] if last else [key_sums]), 16,
            scratch=[pltpu.VMEM(*key_sums)] if last else [],
        )

    finals = []
    for r in range(4):
        if r == 0:
            crossed_only = lambda x, c, y, z: (1 - x, c, y, z) if y != c else None
            other = pick(own_other, send(w_rest, crossed_only), thin)
        else:
            other = send(rests[r], over_x)
        split = r == 3
        groups = ((0,), (1,)) if split else ((0, 1),)
        carry = []
        dqs = []
        for which in groups:
            weights = [(rests[r], other)[i] for i in which]
            if r == 0 or r == 3 and which == (1,):
                (give,) = part(r, which, weights, ("give",))
                (keep,) = part(r, which, weights, ("keep",))
            else:
                give, keep = part(r, which, weights, ("give", "keep"))
            back = send(give, over_y)
            dq, near, *far = grads(r, which, keep, back, carry)
            carry = [near] + far
            dqs.append(dq)
        if not split:
            from_far = send(far[0], over_x)
            ours, crossed = near_call(
                merge_kernel, info, dqs + [near, from_far], [((rows, 512), BF)] * 2, 8
            )
            finals += [ours, send(crossed, over_core)]

    far_mine = send(far[0], over_x)
    far_theirs = send(far[1], over_x_and_core)
    (crossed,) = near_call(cross_kernel, info, dqs + [near], [((rows, 512), BF)], 8)
    crossed = send(crossed, over_core)
    partial = near_call(
        finish_kernel, info, finals, [(a.shape, BF) for a in (q, k, v)], 16, out_hbm=True
    )
    vmem = pl.BlockSpec(memory_space=pltpu.VMEM)
    hbm = pl.BlockSpec(memory_space=pltpu.HBM)
    held = [
        pltpu.with_memory_space_constraint(a, pltpu.VMEM)
        for a in dqs + [near, crossed, far_mine, far_theirs]
    ]
    outs = pl.pallas_call(
        last_kernel,
        in_specs=[pl.BlockSpec(memory_space=pltpu.SMEM)] + [vmem] * 6 + [hbm] * 3,
        out_specs=[hbm] * 3,
        out_shape=[jax.ShapeDtypeStruct(a.shape, BF) for a in (q, k, v)],
        scratch_shapes=[pltpu.VMEM((rows, 512), BF)] * 2 + [dma((6,))],
        input_output_aliases={7: 0, 8: 1, 9: 2},
        compiler_params=pltpu.CompilerParams(vmem_limit_bytes=8 * 1024 * 1024),
        name="L",
    )(info, *held, *partial)
    return tuple(a[None] for a in outs)


def fits_fast(mesh):
    return dict(mesh.shape) == {"dp": 8, "ctx": 4}


def chosen_body(mesh):
    def run(queries, projected_keys, projected_values, attention_result, output_grad, out_weight):
        fast = (
            fits_fast(mesh)
            and queries.shape == (1, 256, 2048)
            and out_weight.shape[0] == 256
            and projected_keys.shape == (1, 256, 1024)
            and output_grad.shape[2] % 256 == 0
            and output_grad.shape[2] // 2 > SHARED_COLS
        )
        use = fast_body if fast else body
        return use(
            queries, projected_keys, projected_values, attention_result, output_grad, out_weight
        )

    return run


def solution(mesh):
    placed = (
        P("dp", "ctx", None),
        P("dp", "ctx", None),
        P("dp", "ctx", None),
        P("dp", "ctx", None),
        P("dp", "ctx", None),
        P("dp", None),
    )
    step = jax.shard_map(
        chosen_body(mesh),
        mesh=mesh,
        in_specs=placed,
        out_specs=(P("dp", "ctx", None), P("dp", "ctx", None), P("dp", "ctx", None)),
        check_vma=False,
    )
    if not fits_fast(mesh):
        return step
    return step
```
